32 devices in a mesh: wave: 4 (over y, core), lev: 8 (over z, x).
Axes of the slice: x: 2, y: 2, z: 4, core: 2. Of those that a mesh axis runs over, the one named last changes fastest.
Arguments:
- spectral: bfloat16 [8, 6, 1280, 1280], P('lev', None, 'wave'), may hold values from -0.16992188 to 0.16992188
- legendre: bfloat16 [1280, 6, 1280], P('wave'), may hold values from -0.15625 to 0.15625
- slot_wave: int32 [1280], replicated, may hold values from 0 to 1279, each once
- cycle_len: int32 [6], replicated, may hold values from 2576 to 5136, as said below
- lat_order: int32 [12], replicated, may hold values from 0 to 11, each once
Outputs:
- grid: float32 [12, 124416], P('wave', 'lev')
The draws below stay inside these ranges and needn't reach their ends.
Inputs may be any that keep to these rules, and one draw needn't show every extreme that they name: `slot_wave`: each wavenumber is held in exactly one slot. `lat_order`: each latitude is held in exactly one row. `cycle_len`: every cycle length is a multiple of 16; some pair has exactly 5136 points and some pair exactly 2576.
All inputs are finite; a program needn't handle non-finite values.
Results may differ from the reference program's by a relative error of at most 0.0003.
Values sent between devices are 32-bit elements; how exact they have to be, the bound alone decides.
A program may use at most 64 MiB of HBM per device.

```python
import math
import jax
import jax.numpy as jnp
from jax import lax

MMAX = 1280
NDEG = 1280
RMAX = 5136
FIELDS = 3
LEVELS = 8
LATW = 12
LATH = 6
RPAD = 5184


def draw_cycle_len(key, part):
    first_key = jax.random.fold_in(key, 11)
    second_key = jax.random.fold_in(key, 12)
    third_key = jax.random.fold_in(key, 13)
    steps_count = (RMAX - (2 * MMAX + 16)) // 16 + 1
    offsets = jax.random.randint(first_key, (LATH,), 0, steps_count)
    lengths = RMAX - 16 * offsets
    longest = jax.random.randint(second_key, (), 0, LATH)
    shortest = (longest + 1 + jax.random.randint(third_key, (), 0, LATH - 1)) % LATH
    positions = jnp.arange(LATH, dtype=jnp.int32)
    lengths = jnp.where(positions == longest, RMAX, lengths)
    lengths = jnp.where(positions == shortest, 2 * MMAX + 16, lengths)
    return lengths.astype(jnp.int32)


def level_of(own_key, shape, pieces, low, top_value):
    level, own = 1.0, jax.random.fold_in(own_key, 6)
    for dim, blocks in pieces:
        draws = jnp.exp(jax.random.uniform(jax.random.fold_in(own, dim), (blocks,), jnp.float32, low / len(pieces), top_value / len(pieces)))
        level = level * jnp.repeat(draws, shape[dim] // blocks).reshape([-1 if axis == dim else 1 for axis in range(len(shape))])
    return level


def centred(stream_key, shape, spread, bound, cuts=(), kind=jnp.bfloat16):
    entries = jax.random.normal(stream_key, shape, jnp.float32) * spread
    if len(cuts) > 0:
        entries = level_of(stream_key, shape, cuts, -0.22, 0.18) * entries
    return jnp.clip(entries, min=-bound, max=bound).astype(kind)


def setup_inputs(seed: int = 0) -> dict:
    streams_of = jax.random.split(jax.random.key(seed), 6)
    spectral = centred(streams_of[0], (LEVELS, 2 * FIELDS, MMAX, NDEG), 0.028, 0.16992188, ((0, 8), (2, 4)))
    legendre = centred(streams_of[1], (MMAX, LATH, NDEG), NDEG ** -0.5, 0.15625, ((0, 4),))
    slot_wave = jax.random.permutation(streams_of[2], MMAX).astype(jnp.int32)
    cycle_len = draw_cycle_len(jax.random.fold_in(streams_of[5], 71), 0)
    lat_order = jax.random.permutation(streams_of[4], LATW).astype(jnp.int32)
    return dict(spectral=spectral, legendre=legendre, slot_wave=slot_wave, cycle_len=cycle_len, lat_order=lat_order)


def cycle_tables(length, count_points):
    waves = jnp.arange(MMAX, dtype=jnp.int32).reshape(MMAX // 16, 16)
    points = jnp.arange(count_points, dtype=jnp.int32)
    phases = (waves[:, :, None] * points[None, None, :]) % length
    angles = (2.0 * math.pi) * phases.astype(jnp.float32) / length.astype(jnp.float32)
    weights = jnp.where(waves == 0, 1.0, 2.0).astype(jnp.float32)[:, :, None]
    return weights * jnp.cos(angles), weights * jnp.sin(angles)


def twiddle():
    residues = jnp.arange(16, dtype=jnp.int32)
    angles = (2.0 * math.pi / 16.0) * ((residues[:, None] * residues[None, :]) % 16).astype(jnp.float32)
    return jnp.cos(angles), jnp.sin(angles)


def place_points(folded, length):
    columns = folded.shape[-1]
    flattened = folded.reshape(folded.shape[:-2] + (16 * columns,))
    points = jnp.arange(RPAD, dtype=jnp.int32)
    period = length // 16
    position = jnp.minimum(points // period, 15) * columns + points % period
    gathered = jnp.take(flattened, position, axis=-1)
    return jnp.where(points < length, gathered, jnp.float32(0.0))


def fold_cycle(coeffs, length):
    highest = lax.Precision.HIGHEST
    cosine, sine = cycle_tables(length, RMAX // 16)
    real_part = coeffs[:, :, 0]
    imag_part = coeffs[:, :, 1]
    inner_real = jnp.einsum("lfab,abp->lfbp", real_part, cosine, precision=highest) - jnp.einsum("lfab,abp->lfbp", imag_part, sine, precision=highest)
    inner_imag = jnp.einsum("lfab,abp->lfbp", real_part, sine, precision=highest) + jnp.einsum("lfab,abp->lfbp", imag_part, cosine, precision=highest)
    twist_cos, twist_sin = twiddle()
    folded = jnp.einsum("lfbp,bq->lfqp", inner_real, twist_cos, precision=highest) - jnp.einsum("lfbp,bq->lfqp", inner_imag, twist_sin, precision=highest)
    return place_points(folded, length)


def legendre_block(inputs):
    spec_block, table_block, wave_block = inputs
    degree = jnp.arange(NDEG, dtype=jnp.int32)
    live_mask = degree[None, :] >= wave_block[:, None]
    even_mask = ((degree[None, :] + wave_block[:, None]) % 2) == 0
    coeffs = spec_block.astype(jnp.float32)
    nothing = jnp.zeros_like(coeffs)
    even_part = jnp.where((live_mask & even_mask)[None, None], coeffs, nothing)
    odd_part = jnp.where((live_mask & jnp.logical_not(even_mask))[None, None], coeffs, nothing)
    tables = table_block.astype(jnp.float32)
    highest = lax.Precision.HIGHEST
    sym_part = jnp.einsum("xcsn,skn->xcsk", even_part, tables, precision=highest)
    anti_part = jnp.einsum("xcsn,skn->xcsk", odd_part, tables, precision=highest)
    return jnp.concatenate([sym_part + anti_part, sym_part - anti_part], axis=3)


def reference(spectral, legendre, slot_wave, cycle_len, lat_order):
    blocks = 16
    width_block = MMAX // blocks
    spec_blocks = jnp.moveaxis(spectral.reshape(LEVELS, 2 * FIELDS, blocks, width_block, NDEG), 2, 0)
    table_blocks = legendre.reshape(blocks, width_block, LATH, NDEG)
    wave_blocks = slot_wave.reshape(blocks, width_block)
    fourier = lax.map(legendre_block, (spec_blocks, table_blocks, wave_blocks))
    fourier = jnp.moveaxis(fourier, 0, 2).reshape(LEVELS, 2 * FIELDS, MMAX, LATW)
    slots = jnp.arange(MMAX, dtype=jnp.int32)
    inverse = jnp.zeros((MMAX,), jnp.int32).at[slot_wave].set(slots)
    fourier_m = jnp.take(fourier, inverse, axis=2)

    def one_row(row):
        latitude = lat_order[row]
        length = cycle_len[latitude % LATH]
        coeffs = lax.dynamic_index_in_dim(fourier_m, latitude, axis=3, keepdims=False)
        coeffs = coeffs.reshape(LEVELS, FIELDS, 2, MMAX // 16, 16)
        placed = fold_cycle(coeffs, length)
        return jnp.transpose(placed.reshape(LEVELS * FIELDS, RPAD)).reshape(RPAD * LEVELS * FIELDS)

    return lax.map(one_row, jnp.arange(LATW, dtype=jnp.int32))
```

```python
import functools
import math

import jax
import jax.numpy as jnp
from jax import lax
from jax.experimental import pallas as pl
from jax.experimental.pallas import tpu as pltpu
from jax.sharding import PartitionSpec as P

RMAX = 5136
LANES = 128
BLOCK = 16


def split(value):
    high = value.astype(jnp.bfloat16)
    return high, (value - high.astype(jnp.float32)).astype(jnp.bfloat16)


def dot_nt(left, right):
    return lax.dot_general(left, right, (((1,), (1,)), ((), ())), preferred_element_type=jnp.float32)


def turns(t):
    y = math.pi * t
    z = y * y
    sine = jnp.full_like(z, 1.0 / math.factorial(13))
    for n in (11, 9, 7, 5, 3, 1):
        sign = -1.0 if (n // 2) % 2 else 1.0
        sine = sine * z + sign / math.factorial(n)
    sine = sine * y
    cosine = jnp.full_like(z, 1.0 / math.factorial(12))
    for n in (10, 8, 6, 4, 2, 0):
        sign = -1.0 if (n // 2) % 2 else 1.0
        cosine = cosine * z + sign / math.factorial(n)
    return 1.0 - 2.0 * sine * sine, 2.0 * sine * cosine


def iota(shape, dim):
    return lax.broadcasted_iota(jnp.int32, shape, dim)


def kernel(
    half_step, chunk,
    wave_ref, lat_ref, cycle_ref, spec_hbm, leg_hbm, out_ref,
    spec_ref, leg_ref, col_ref, four_ref, wsend_ref, wgot_ref,
    twist_ref, cen_ref, tab_ref, u_ref, place_ref, send_ref, got_ref,
    load_sem, wown_sem, wsend_sem, wrecv_sem, own_sem, send_sem, recv_sem,
):
    parts, slot_count, degrees = spec_ref.shape
    half_cycles = leg_ref.shape[0]
    fields = parts // 2
    groups, wave_count, cycles = wsend_ref.shape[:3]
    lev_count = send_ref.shape[1]
    wide = send_ref.shape[-1]
    slots = wave_ref.shape[0]
    tiles = slots // LANES
    step = 2 * half_step
    points_dev = 4 * step
    half_rows = twist_ref.shape[2]
    blocks = half_rows // 8
    counts = (half_step + 15) // 16
    low_at = tab_ref.shape[2] - 16 * counts
    me = lax.axis_index("lev")
    my_wave = lax.axis_index("wave")
    first_row = my_wave * cycles

    barrier = pltpu.get_barrier_semaphore()
    for offset in range(1, lev_count):
        peer = lax.rem(me + offset, lev_count)
        pl.semaphore_signal(barrier, inc=1, device_id={"lev": peer}, device_id_type=pl.DeviceIdType.MESH)
    for offset in range(1, wave_count):
        peer = lax.rem(my_wave + offset, wave_count)
        pl.semaphore_signal(barrier, inc=1, device_id={"wave": peer}, device_id_type=pl.DeviceIdType.MESH)

    loads = []
    for i in range(slot_count // chunk):
        at = pl.ds(i * chunk, chunk)
        pair = [
            pltpu.make_async_copy(leg_hbm.at[:, at], leg_ref.at[:, at], load_sem.at[0, i]),
            pltpu.make_async_copy(spec_hbm.at[:, at], spec_ref.at[:, at], load_sem.at[1, i]),
        ]
        for copy in pair:
            copy.start()
        loads.append(pair)

    waves = wave_ref[...].reshape(1, slots).astype(jnp.float32)

    mine = pltpu.roll(waves, slots - my_wave * slot_count, 1)
    eye = iota((LANES, LANES), 0) == iota((LANES, LANES), 1)
    for g in range(groups):
        column = jnp.sum(jnp.where(eye, mine[:, g * LANES : (g + 1) * LANES], 0.0), axis=1, keepdims=True)
        col_ref[g * LANES : (g + 1) * LANES] = jnp.broadcast_to(column, (LANES, LANES))

    near = [i + 0.5 for i in range(8)]
    twist = [step * (i + 0.5) for i in range(8)]
    rest = [16.0 * k + 8.0 for k in range(counts)] + [8.0 * step * a for a in range(1, blocks)]
    rest += [(lev_count * points_dev - 1) / 2]
    rest_count = len(rest)
    rest_rows = (rest_count + 7) // 8 * 8
    row = iota((rest_rows, 1), 0)
    row8 = iota((8, 1), 0).astype(jnp.float32) + 0.5
    rest_mult = jnp.zeros((rest_rows, 1), jnp.float32)
    for i, value in enumerate(rest):
        rest_mult = jnp.where(row == i, value, rest_mult)
    mult = jnp.concatenate([row8, row8 * step, rest_mult], axis=0)
    lengths = [
        cycle_ref[lat_ref[first_row + r] % half_cycles].astype(jnp.float32) for r in range(cycles)
    ]
    if low_at > 16 * counts:
        hole = low_at - 16 * counts
        tab_ref[:, :, 16 * counts : low_at] = jnp.zeros((cycles, 2, hole, slots), jnp.bfloat16)

    def tables(r, t):
        at = slice(t * LANES, (t + 1) * LANES)
        wave = waves[:, at]
        length = lengths[r]
        inverse = 1.0 / jnp.full((1, LANES), length)
        phase = wave * mult
        whole = jnp.floor(phase * inverse + 0.5)
        cosine, sine = turns((phase - whole * length) * inverse)
        nc, ns, tc, ts = cosine[0:8], sine[0:8], cosine[8:16], sine[8:16]
        rc, rs = cosine[16:], sine[16:]
        twist_ref[r, 0, 0:8, at] = tc
        twist_ref[r, 1, 0:8, at] = ts
        for a in range(1, blocks):
            i = counts + a - 1
            c, s = rc[i : i + 1], rs[i : i + 1]
            twist_ref[r, 0, 8 * a : 8 * a + 8, at] = tc * c - ts * s
            twist_ref[r, 1, 8 * a : 8 * a + 8, at] = ts * c + tc * s
        weight = jnp.where(wave == 0.0, 1.0, 2.0)
        i = rest_count - 1
        cen_ref[r, 0:1, at] = rc[i : i + 1] * weight
        cen_ref[r, 1:2, at] = rs[i : i + 1] * weight
        for k in range(counts):
            c, s = rc[k : k + 1], rs[k : k + 1]
            cc, ss, sc, cs = c * nc, s * ns, s * nc, c * ns
            for which, value in (
                (0, jnp.concatenate([cc + ss, cc - ss], axis=0)),
                (1, jnp.concatenate([sc - cs, sc + cs], axis=0)),
            ):
                high, low = split(value)
                tab_ref[r, which, 16 * k : 16 * k + 16, at] = high
                tab_ref[r, which, low_at + 16 * k : low_at + 16 * k + 16, at] = low

    chunks = LANES // BLOCK
    lane = iota((1, LANES), 1)
    lane_chunk = lane // BLOCK
    degree = iota((BLOCK, degrees), 1)
    flip = jnp.where((iota((BLOCK, degrees), 1) & 1) == 1, -1.0, 1.0).astype(jnp.bfloat16)
    own = iota((BLOCK, LANES), 0) == iota((BLOCK, LANES), 1) % BLOCK
    lats = 2 * half_cycles

    def legendre(b, turn):
        at = slice(b * BLOCK, (b + 1) * BLOCK)
        column = col_ref[at, 0:1].astype(jnp.int32)
        live = jnp.where(degree >= column, 1.0, 0.0).astype(jnp.bfloat16)
        north = leg_ref[:, at, :] * live[None]
        south = north * flip[None]
        table = jnp.concatenate([north, south], axis=0).reshape(lats * BLOCK, degrees)
        order = [(j - turn) % chunks for j in range(chunks)]
        rows = jnp.concatenate([spec_ref[c if c < parts else 0, at, :] for c in order], axis=0)
        product = dot_nt(table, rows).reshape(lats, BLOCK, LANES)
        return jnp.sum(jnp.where(own[None], product, 0.0), axis=1)

    wave_copies = []

    def send_group(g, sums):
        sign = jnp.where(
            (iota((lats, 1), 0) >= half_cycles)
            & ((mine[:, g * LANES : (g + 1) * LANES].astype(jnp.int32) & 1) == 1),
            -1.0,
            1.0,
        )
        for c in range(parts):
            picked = sums[0]
            for b in range(1, len(sums)):
                picked = jnp.where(lane_chunk == (c + b) % chunks, sums[b], picked)
            if c:
                picked = pltpu.roll(picked, LANES - c * BLOCK, 1)
            four_ref[:, (c % 2) * 4 + c // 2, :] = picked * sign
        for w in range(wave_count):
            for r in range(cycles):
                wsend_ref[g, w, r] = four_ref[lat_ref[w * cycles + r]]
        if g == 0:
            pl.semaphore_wait(barrier, lev_count + wave_count - 2)
        for offset in range(1, wave_count):
            peer = lax.rem(my_wave + offset, wave_count)
            copy = pltpu.make_async_remote_copy(
                src_ref=wsend_ref.at[g, peer],
                dst_ref=wgot_ref.at[g, my_wave],
                send_sem=wsend_sem.at[g, offset],
                recv_sem=wrecv_sem.at[g, offset],
                device_id={"wave": peer},
                device_id_type=pl.DeviceIdType.MESH,
            )
            copy.start()
            wave_copies.append(copy)
        kept = pltpu.make_async_copy(wsend_ref.at[g, my_wave], wgot_ref.at[g, my_wave], wown_sem.at[g])
        kept.start()
        wave_copies.append(kept)

    todo = [(r, t) for r in range(cycles) for t in range(tiles)]
    ahead = todo[: 2 * tiles]
    total_blocks = slot_count // BLOCK
    done = 0
    sums = []
    for b in range(total_blocks):
        if b * BLOCK % chunk == 0:
            for copy in loads[b * BLOCK // chunk]:
                copy.wait()
        sums.append(legendre(b, b % chunks))
        if b % chunks == chunks - 1 or b == total_blocks - 1:
            send_group(b // chunks, sums)
            sums = []
        upto = len(ahead) * (b + 1) // total_blocks
        for r, t in ahead[done:upto]:
            tables(r, t)
        done = upto
    for r, t in todo[2 * tiles :]:
        tables(r, t)

    group = lev_count * fields
    span = half_step * group
    source = iota((wide, 1), 0)
    target = jnp.where(source < fields * half_step, (source % half_step) * group + source // half_step, -1)
    for j in range(place_ref.shape[1] // LANES):
        at = slice(j * LANES, (j + 1) * LANES)
        place_ref[:, at] = jnp.where(iota((wide, LANES), 1) + j * LANES == target, 1.0, 0.0).astype(jnp.bfloat16)

    picks = {}
    for f in range(fields):
        point = (lane + (LANES - f * half_step % LANES)) % LANES
        for back in (0, 1):
            p = half_step - 1 - point if back else point
            p = jnp.clip(p, 0, half_step - 1)
            low = p % 16
            index = p - low + jnp.where(low < 8, 7 - low, low)
            picks[f, back] = jnp.broadcast_to(index, (half_rows, LANES))
    where_lane = iota((8, wide), 1)
    where_row = iota((8, wide), 0)
    inside = jnp.where(where_lane < fields * half_step, where_lane % half_step, 1 << 20)
    reach = {}
    for upper in (0, 1):
        i = where_row % 4 if upper else 3 - where_row % 4
        reach[upper] = (step * i + half_step * (where_row // 4) + inside).astype(jnp.float32)

    for copy in wave_copies:
        copy.wait()

    copies = []
    turn_sign = jnp.where(iota((8, 1), 0) < 4, -1.0, 1.0)
    for r in range(cycles):
        for t in range(tiles):
            at = slice(t * LANES, (t + 1) * LANES)
            coef = None
            position = t * LANES
            while position < (t + 1) * LANES:
                w, inner = position // slot_count, position % slot_count
                g, start = inner // LANES, inner % LANES
                size = min((t + 1) * LANES - position, slot_count - inner, LANES - start)
                piece = wgot_ref[g, w, r]
                to = position - t * LANES
                if to != start:
                    piece = pltpu.roll(piece, (to - start) % LANES, 1)
                coef = piece if coef is None else jnp.where(lane >= to, piece, coef)
                position += size
            coef = coef * cen_ref[r, 0:1, at] + pltpu.roll(coef, 4, 0) * (cen_ref[r, 1:2, at] * turn_sign)
            tc, ts = twist_ref[r, 0, :, at], twist_ref[r, 1, :, at]
            for f in range(fields):
                real, imag = coef[f : f + 1], coef[4 + f : 5 + f]
                for which, first, value in ((0, 0, real * tc), (0, 1, imag * ts), (1, 0, real * ts), (1, 1, imag * tc)):
                    high, low = split(value)
                    base = (first * fields + f) * half_rows
                    u_ref[which, base : base + half_rows, at] = high
                    base += 2 * fields * half_rows
                    u_ref[which, base : base + half_rows, at] = low
        both = []
        rows = 2 * fields * half_rows
        for which in (0, 1):
            product = dot_nt(u_ref[which], tab_ref[r, which])
            value = product[:rows] + product[rows:]
            both.append(value[:, :LANES] + jnp.concatenate([value[:, low_at:], jnp.zeros((rows, low_at - 16 * counts), jnp.float32)], axis=1))
        mixed = {}
        for f in range(fields):
            p1, p2 = (both[0][(i * fields + f) * half_rows : (i * fields + f + 1) * half_rows] for i in (0, 1))
            p3, p4 = (both[1][(i * fields + f) * half_rows : (i * fields + f + 1) * half_rows] for i in (0, 1))
            even_up, odd_up = p1 - p2, p3 + p4
            even_down, odd_down = p1 + p2, p4 - p3
            for upper, even, odd in ((1, even_up, odd_up), (0, even_down, odd_down)):
                for back, value in ((0, even - odd), (1, even + odd)):
                    mixed[upper, back, f] = jnp.take_along_axis(
                        value, picks[f, back], axis=1, mode="promise_in_bounds"
                    )
        for upper in (0, 1):
            row_tiles = []
            for back in (1, 0):
                pieces = []
                for j in range(wide // LANES):
                    piece = None
                    for f in range(fields):
                        start, stop = f * half_step - j * LANES, (f + 1) * half_step - j * LANES
                        if stop <= 0 or start >= LANES:
                            continue
                        value = mixed[upper, back, f]
                        piece = value if piece is None else jnp.where(lane >= start, value, piece)
                    pieces.append(piece)
                row_tiles.append(jnp.concatenate(pieces, axis=1))
            for a in range(lev_count // 2):
                dest = lev_count // 2 + a if upper else lev_count // 2 - 1 - a
                tile = jnp.concatenate([value[4 * a : 4 * a + 4] for value in row_tiles], axis=0)
                send_ref[r, dest] = jnp.where(reach[upper] < lengths[r] - float(points_dev * dest), tile, 0.0)
        started = []
        offsets = sorted(range(1, lev_count), key=lambda o: abs(o - lev_count / 2))
        for offset in offsets:
            peer = lax.rem(me + offset, lev_count)
            copy = pltpu.make_async_remote_copy(
                src_ref=send_ref.at[r, peer],
                dst_ref=got_ref.at[r, me],
                send_sem=send_sem.at[r, offset],
                recv_sem=recv_sem.at[r, offset],
                device_id={"lev": peer},
                device_id_type=pl.DeviceIdType.MESH,
            )
            copy.start()
            started.append(copy)
        kept = pltpu.make_async_copy(send_ref.at[r, me], got_ref.at[r, me], own_sem.at[r])
        kept.start()
        started.append(kept)
        copies.append(started)

    upper = me >= lev_count // 2
    sub = iota((8, place_ref.shape[1]), 0)
    order = jnp.where(upper, sub, (sub // 4) * 4 + 3 - sub % 4)
    for r in range(cycles):
        for copy in copies[r]:
            copy.wait()
        high, low = split(got_ref[r].reshape(lev_count * 8, wide))
        spread = jnp.dot(high, place_ref[...], preferred_element_type=jnp.float32) + jnp.dot(
            low, place_ref[...], preferred_element_type=jnp.float32
        )
        total = spread[:8]
        for level in range(1, lev_count):
            total = total + pltpu.roll(spread[level * 8 : (level + 1) * 8], fields * level, 1)
        total = jnp.take_along_axis(total, order, axis=0, mode="promise_in_bounds")
        for q in range(8):
            s = (q % 2) * 4 + q // 2
            out_ref[r : r + 1, q * span : (q + 1) * span] = total[s : s + 1, :span]


def local(spectral, legendre, slot_wave, cycle_len, lat_order):
    slot_count = spectral.shape[2]
    degrees = spectral.shape[3]
    half_cycles = legendre.shape[1]
    lev_count = lax.axis_size("lev")
    wave_count = lax.axis_size("wave")
    slots = slot_wave.shape[0]
    padded_len = (RMAX + 8 * lev_count - 1) // (8 * lev_count) * 8 * lev_count
    points_dev = padded_len // lev_count
    half_step = points_dev // 8
    parts = spectral.shape[0] * spectral.shape[1]
    fields = parts // 2
    cycles = lat_order.shape[0] // wave_count
    groups = (slot_count + LANES - 1) // LANES
    chunk = 32 if slot_count % 32 == 0 else 16
    half_rows = 2 * lev_count
    counts = (half_step + 15) // 16
    low_at = (16 * counts + LANES - 1) // LANES * LANES

    wide = (fields * half_step + LANES - 1) // LANES * LANES
    span = (fields * lev_count * half_step + LANES - 1) // LANES * LANES
    smem = pl.BlockSpec(memory_space=pltpu.SMEM)
    vmem = pl.BlockSpec(memory_space=pltpu.VMEM)
    hbm = pl.BlockSpec(memory_space=pl.ANY)
    return pl.pallas_call(
        functools.partial(kernel, half_step, chunk),
        out_shape=pltpu.VMEM((cycles, points_dev * lev_count * fields), jnp.float32),
        in_specs=[vmem, smem, smem, hbm, hbm],
        out_specs=vmem,
        scratch_shapes=[
            pltpu.VMEM((parts, slot_count, degrees), jnp.bfloat16),
            pltpu.VMEM((half_cycles, slot_count, degrees), jnp.bfloat16),
            pltpu.VMEM((groups * LANES, LANES), jnp.float32),
            pltpu.VMEM((2 * half_cycles, 8, LANES), jnp.float32),
            pltpu.VMEM((groups, wave_count, cycles, 8, LANES), jnp.float32),
            pltpu.VMEM((groups, wave_count, cycles, 8, LANES), jnp.float32),
            pltpu.VMEM((cycles, 2, half_rows, slots), jnp.float32),
            pltpu.VMEM((cycles, 8, slots), jnp.float32),
            pltpu.VMEM((cycles, 2, low_at + 16 * counts, slots), jnp.bfloat16),
            pltpu.VMEM((2, 4 * fields * half_rows, slots), jnp.bfloat16),
            pltpu.VMEM((wide, span), jnp.bfloat16),
            pltpu.VMEM((cycles, lev_count, 8, wide), jnp.float32),
            pltpu.VMEM((cycles, lev_count, 8, wide), jnp.float32),
            pltpu.SemaphoreType.DMA((2, slot_count // chunk)),
            pltpu.SemaphoreType.DMA((groups,)),
            pltpu.SemaphoreType.DMA((groups, wave_count)),
            pltpu.SemaphoreType.DMA((groups, wave_count)),
            pltpu.SemaphoreType.DMA((cycles,)),
            pltpu.SemaphoreType.DMA((cycles, lev_count)),
            pltpu.SemaphoreType.DMA((cycles, lev_count)),
        ],
        compiler_params=pltpu.CompilerParams(collective_id=0, has_side_effects=True),
        name="transform",
    )(
        slot_wave, lat_order, cycle_len,
        spectral.reshape(parts, slot_count, degrees), jnp.transpose(legendre, (1, 0, 2)),
    )


def solution(mesh):
    in_specs = (P("lev", None, "wave", None), P("wave", None, None), P(), P(), P())
    out_specs = P("wave", "lev")
    return jax.shard_map(local, mesh=mesh, in_specs=in_specs, out_specs=out_specs, check_vma=False)
```

```python
import functools
import math

import jax
import jax.numpy as jnp
from jax import lax
from jax.experimental import pallas as pl
from jax.experimental.pallas import tpu as pltpu
from jax.sharding import PartitionSpec as P

RMAX = 5136
LANES = 128
BLOCK = 16


def split(value):
    high = value.astype(jnp.bfloat16)
    return high, (value - high.astype(jnp.float32)).astype(jnp.bfloat16)


def dot_nt(left, right):
    return lax.dot_general(left, right, (((1,), (1,)), ((), ())), preferred_element_type=jnp.float32)


def turns(t):
    y = math.pi * t
    z = y * y
    sine = jnp.full_like(z, 1.0 / math.factorial(13))
    for n in (11, 9, 7, 5, 3, 1):
        sign = -1.0 if (n // 2) % 2 else 1.0
        sine = sine * z + sign / math.factorial(n)
    sine = sine * y
    cosine = jnp.full_like(z, 1.0 / math.factorial(12))
    for n in (10, 8, 6, 4, 2, 0):
        sign = -1.0 if (n // 2) % 2 else 1.0
        cosine = cosine * z + sign / math.factorial(n)
    return 1.0 - 2.0 * sine * sine, 2.0 * sine * cosine


def iota(shape, dim):
    return lax.broadcasted_iota(jnp.int32, shape, dim)


def kernel(
    half_step, chunk,
    wave_ref, lat_ref, cycle_ref, spec_hbm, leg_hbm, out_ref,
    spec_ref, leg_ref, col_ref, four_ref, wsend_ref, wgot_ref,
    twist_ref, cen_ref, tab_ref, place_ref, send_ref, got_ref,
    load_sem, wown_sem, wsend_sem, wrecv_sem, own_sem, send_sem, recv_sem,
):
    parts, slot_count, degrees = spec_ref.shape
    half_cycles = leg_ref.shape[0]
    fields = parts // 2
    groups, wave_count, cycles = wsend_ref.shape[:3]
    lev_count = send_ref.shape[1]
    wide = send_ref.shape[-1]
    slots = wave_ref.shape[0]
    tiles = slots // LANES
    step = 2 * half_step
    points_dev = 4 * step
    half_rows = twist_ref.shape[2]
    blocks = half_rows // 8
    counts = (half_step + 15) // 16
    low_at = tab_ref.shape[3] - 16 * counts
    me = lax.axis_index("lev")
    my_wave = lax.axis_index("wave")
    first_row = my_wave * cycles

    barrier = pltpu.get_barrier_semaphore()
    for offset in range(1, lev_count):
        peer = lax.rem(me + offset, lev_count)
        pl.semaphore_signal(barrier, inc=1, device_id={"lev": peer}, device_id_type=pl.DeviceIdType.MESH)
    for offset in range(1, wave_count):
        peer = lax.rem(my_wave + offset, wave_count)
        pl.semaphore_signal(barrier, inc=1, device_id={"wave": peer}, device_id_type=pl.DeviceIdType.MESH)

    loads = []
    for i in range(slot_count // chunk):
        at = pl.ds(i * chunk, chunk)
        pair = [
            pltpu.make_async_copy(leg_hbm.at[:, at], leg_ref.at[:, at], load_sem.at[0, i]),
            pltpu.make_async_copy(spec_hbm.at[:, at], spec_ref.at[:, at], load_sem.at[1, i]),
        ]
        for copy in pair:
            copy.start()
        loads.append(pair)

    waves = wave_ref[...].reshape(1, slots).astype(jnp.float32)

    mine = pltpu.roll(waves, slots - my_wave * slot_count, 1)
    eye = iota((LANES, LANES), 0) == iota((LANES, LANES), 1)
    for g in range(groups):
        column = jnp.sum(jnp.where(eye, mine[:, g * LANES : (g + 1) * LANES], 0.0), axis=1, keepdims=True)
        col_ref[g * LANES : (g + 1) * LANES] = column - iota((LANES, LANES), 1).astype(jnp.float32)

    near = [i + 0.5 for i in range(8)]
    twist = [step * (i + 0.5) for i in range(8)]
    rest = [16.0 * k + 8.0 for k in range(counts)] + [8.0 * step * a for a in range(1, blocks)]
    rest += [(lev_count * points_dev - 1) / 2]
    rest_count = len(rest)
    rest_rows = (rest_count + 7) // 8 * 8
    row = iota((rest_rows, 1), 0)
    row8 = iota((8, 1), 0).astype(jnp.float32) + 0.5
    rest_mult = jnp.zeros((rest_rows, 1), jnp.float32)
    for i, value in enumerate(rest):
        rest_mult = jnp.where(row == i, value, rest_mult)
    mult = jnp.concatenate([row8, row8 * step, rest_mult], axis=0)
    lengths = [
        cycle_ref[lat_ref[first_row + r] % half_cycles].astype(jnp.float32) for r in range(cycles)
    ]
    if low_at > 16 * counts:
        hole = low_at - 16 * counts
        tab_ref[:, :, :, 16 * counts : low_at, :] = jnp.zeros((cycles, 2, tiles, hole, LANES), jnp.bfloat16)

    def tables(r, t):
        at = slice(t * LANES, (t + 1) * LANES)
        wave = waves[:, at]
        length = lengths[r]
        inverse = 1.0 / jnp.full((1, LANES), length)
        phase = wave * mult
        whole = jnp.floor(phase * inverse + 0.5)
        cosine, sine = turns((phase - whole * length) * inverse)
        nc, ns, tc, ts = cosine[0:8], sine[0:8], cosine[8:16], sine[8:16]
        rc, rs = cosine[16:], sine[16:]
        twist_ref[r, 0, 0:8, at] = tc
        twist_ref[r, 1, 0:8, at] = ts
        for a in range(1, blocks):
            i = counts + a - 1
            c, s = rc[i : i + 1], rs[i : i + 1]
            twist_ref[r, 0, 8 * a : 8 * a + 8, at] = tc * c - ts * s
            twist_ref[r, 1, 8 * a : 8 * a + 8, at] = ts * c + tc * s
        weight = jnp.where(wave == 0.0, 1.0, 2.0)
        i = rest_count - 1
        cen_ref[r, 0:1, at] = rc[i : i + 1] * weight
        cen_ref[r, 1:2, at] = rs[i : i + 1] * weight
        for k in range(counts):
            c, s = rc[k : k + 1], rs[k : k + 1]
            cc, ss, sc, cs = c * nc, s * ns, s * nc, c * ns
            for which, value in (
                (0, jnp.concatenate([cc + ss, cc - ss], axis=0)),
                (1, jnp.concatenate([sc - cs, sc + cs], axis=0)),
            ):
                high, low = split(value)
                tab_ref[r, which, t, 16 * k : 16 * k + 16, :] = high
                tab_ref[r, which, t, low_at + 16 * k : low_at + 16 * k + 16, :] = low

    chunks = LANES // BLOCK
    lane = iota((1, LANES), 1)
    lane_chunk = lane // BLOCK
    flip = jnp.where((iota((BLOCK, degrees), 1) & 1) == 1, -1.0, 1.0).astype(jnp.bfloat16)
    lats = 2 * half_cycles
    own = iota((BLOCK, lats * BLOCK), 0) == iota((BLOCK, lats * BLOCK), 1) % BLOCK

    def legendre(b, turn):
        at = slice(b * BLOCK, (b + 1) * BLOCK)
        column = col_ref[at, :]
        live = jnp.concatenate(
            [jnp.where(column <= float(d), 1.0, 0.0) for d in range(0, degrees, LANES)], axis=1
        ).astype(jnp.bfloat16)
        north = leg_ref[:, at, :] * live[None]
        south = north * flip[None]
        both = (north, south)
        order = [(j - turn) % lats for j in range(lats)]
        table = jnp.concatenate([both[j // half_cycles][j % half_cycles] for j in order], axis=0)
        product = dot_nt(spec_ref[:, at, :].reshape(parts * BLOCK, degrees), table)
        product = product.reshape(parts, BLOCK, lats * BLOCK)
        total = jnp.sum(jnp.where(own[None], product, 0.0), axis=1)
        extra = -total.shape[1] % LANES
        if extra:
            total = jnp.concatenate([total, jnp.zeros((parts, extra), jnp.float32)], axis=1)
        return [total[:, j * LANES : (j + 1) * LANES] for j in range(total.shape[1] // LANES)]

    wave_copies = []

    def send_group(g, sums):
        sign = jnp.where((mine[:, g * LANES : (g + 1) * LANES].astype(jnp.int32) & 1) == 1, -1.0, 1.0)
        for j in range(lats):
            shifts = {}
            for b, total in enumerate(sums):
                place = (j + b) % lats
                shifts.setdefault((b - place) % chunks, []).append((b, place % chunks, total[place // chunks]))
            value = None
            for shift, members in shifts.items():
                picked = None
                for b, at_chunk, total in members:
                    picked = total if picked is None else jnp.where(lane_chunk == at_chunk, total, picked)
                if shift:
                    picked = pltpu.roll(picked, shift * BLOCK, 1)
                first, last = members[0][0], members[-1][0]
                if value is None:
                    value = picked
                else:
                    value = jnp.where((lane_chunk >= first) & (lane_chunk <= last), picked, value)
            if j >= half_cycles:
                value = value * sign
            four_ref[j, 0:parts, :] = value
        for w in range(wave_count):
            for r in range(cycles):
                wsend_ref[g, w, r] = four_ref[lat_ref[w * cycles + r]]
        if g == 0:
            pl.semaphore_wait(barrier, lev_count + wave_count - 2)
        for offset in range(1, wave_count):
            peer = lax.rem(my_wave + offset, wave_count)
            copy = pltpu.make_async_remote_copy(
                src_ref=wsend_ref.at[g, peer],
                dst_ref=wgot_ref.at[g, my_wave],
                send_sem=wsend_sem.at[g, offset],
                recv_sem=wrecv_sem.at[g, offset],
                device_id={"wave": peer},
                device_id_type=pl.DeviceIdType.MESH,
            )
            copy.start()
            wave_copies.append(copy)
        kept = pltpu.make_async_copy(wsend_ref.at[g, my_wave], wgot_ref.at[g, my_wave], wown_sem.at[g])
        kept.start()
        wave_copies.append(kept)

    for t in range(tiles):
        tables(0, t)
    ahead = [(r, t) for r in range(1, min(2, cycles)) for t in range(tiles)]
    total_blocks = slot_count // BLOCK
    done = 0
    sums = []
    for b in range(total_blocks):
        if b * BLOCK % chunk == 0:
            for copy in loads[b * BLOCK // chunk]:
                copy.wait()
        sums.append(legendre(b, b % chunks))
        upto = len(ahead) * (b + 1) // total_blocks
        for r, t in ahead[done:upto]:
            tables(r, t)
        done = upto
        if b % chunks == chunks - 1 or b == total_blocks - 1:
            send_group(b // chunks, sums)
            sums = []
    for r in range(2, cycles):
        for t in range(tiles):
            tables(r, t)

    group = lev_count * fields
    quarter = (half_step + 3) // 4
    source = iota((4 * 64, 1), 0)
    inner = source % 64
    target = jnp.where(
        inner < fields * quarter, (inner % quarter) * group + source // 64 * fields + inner // quarter, -1
    )
    for j in range(place_ref.shape[1] // LANES):
        at = slice(j * LANES, (j + 1) * LANES)
        place_ref[:, at] = jnp.where(iota((4 * 64, LANES), 1) + j * LANES == target, 1.0, 0.0).astype(jnp.bfloat16)

    picks = {}
    inner = lane % 64
    for j in range(2):
        for f in range(fields):
            point = inner - f * quarter
            point = (2 * j + lane // 64) * quarter + jnp.clip(point, 0, quarter - 1)
            for back in (0, 1):
                p = half_step - 1 - point if back else point
                p = jnp.clip(p, 0, half_step - 1)
                low = p % 16
                index = p - low + jnp.where(low < 8, 7 - low, low)
                picks[j, f, back] = jnp.broadcast_to(index, (half_rows, LANES))
    where_lane = iota((8, wide), 1)
    where_row = iota((8, wide), 0)
    inner = where_lane % 64
    inside = where_lane // 64 * quarter + inner % quarter
    inside = jnp.where((inner < fields * quarter) & (inside < half_step), inside, 1 << 20)
    reach = {}
    for upper in (0, 1):
        i = where_row % 4 if upper else 3 - where_row % 4
        reach[upper] = (step * i + half_step * (where_row // 4) + inside).astype(jnp.float32)
    half_lane = lane < 64

    for copy in wave_copies:
        copy.wait()

    copies = []
    odd_row = iota((8, 1), 0) % 2
    turn_sign = jnp.where(odd_row == 1, 1.0, -1.0)
    for r in range(cycles):
        operands = ([], [])
        for t in range(tiles):
            at = slice(t * LANES, (t + 1) * LANES)
            coef = None
            position = t * LANES
            while position < (t + 1) * LANES:
                w, inner = position // slot_count, position % slot_count
                g, start = inner // LANES, inner % LANES
                size = min((t + 1) * LANES - position, slot_count - inner, LANES - start)
                piece = wgot_ref[g, w, r]
                to = position - t * LANES
                if to != start:
                    piece = pltpu.roll(piece, (to - start) % LANES, 1)
                coef = piece if coef is None else jnp.where(lane >= to, piece, coef)
                position += size
            swapped = jnp.where(odd_row == 1, pltpu.roll(coef, 1, 0), pltpu.roll(coef, 7, 0))
            coef = coef * cen_ref[r, 0:1, at] + swapped * (cen_ref[r, 1:2, at] * turn_sign)
            tc, ts = twist_ref[r, 0, :, at], twist_ref[r, 1, :, at]
            pairs = ([], [])
            for first in (0, 1):
                for f in range(fields):
                    part = coef[2 * f + first : 2 * f + first + 1]
                    for which in (0, 1):
                        pairs[which].append(split(part * (tc if which == first else ts)))
            for which in (0, 1):
                operands[which].append(
                    jnp.concatenate([high for high, _ in pairs[which]] + [low for _, low in pairs[which]], axis=0)
                )
        both = []
        rows = 2 * fields * half_rows
        for which in (0, 1):
            table = jnp.concatenate([tab_ref[r, which, t] for t in range(tiles)], axis=1)
            product = dot_nt(jnp.concatenate(operands[which], axis=1), table)
            value = product[:rows] + product[rows:]
            both.append(value[:, :LANES] + jnp.concatenate([value[:, low_at:], jnp.zeros((rows, low_at - 16 * counts), jnp.float32)], axis=1))
        mixed = {}
        for f in range(fields):
            p1, p2 = (both[0][(i * fields + f) * half_rows : (i * fields + f + 1) * half_rows] for i in (0, 1))
            p3, p4 = (both[1][(i * fields + f) * half_rows : (i * fields + f + 1) * half_rows] for i in (0, 1))
            for upper, even, odd in ((1, p1 - p2, p3 + p4), (0, p1 + p2, p4 - p3)):
                for back, value in ((0, even - odd), (1, even + odd)):
                    for j in range(2):
                        mixed[upper, back, j, f] = jnp.take_along_axis(
                            value, picks[j, f, back], axis=1, mode="promise_in_bounds"
                        )
        inner = lane % 64
        for upper in (0, 1):
            row_tiles = []
            for back in (1, 0):
                pieces = []
                for j in range(2):
                    piece = mixed[upper, back, j, 0]
                    for f in range(1, fields):
                        piece = jnp.where(inner >= f * quarter, mixed[upper, back, j, f], piece)
                    pieces.append(piece)
                row_tiles.append(jnp.concatenate(pieces, axis=1))
            for a in range(lev_count // 2):
                dest = lev_count // 2 + a if upper else lev_count // 2 - 1 - a
                tile = jnp.concatenate([value[4 * a : 4 * a + 4] for value in row_tiles], axis=0)
                send_ref[r, dest] = jnp.where(reach[upper] < lengths[r] - float(points_dev * dest), tile, 0.0)
        started = []
        offsets = sorted(range(1, lev_count), key=lambda o: abs(o - lev_count / 2))
        for offset in offsets:
            peer = lax.rem(me + offset, lev_count)
            copy = pltpu.make_async_remote_copy(
                src_ref=send_ref.at[r, peer],
                dst_ref=got_ref.at[r, me],
                send_sem=send_sem.at[r, offset],
                recv_sem=recv_sem.at[r, offset],
                device_id={"lev": peer},
                device_id_type=pl.DeviceIdType.MESH,
            )
            copy.start()
            started.append(copy)
        kept = pltpu.make_async_copy(send_ref.at[r, me], got_ref.at[r, me], own_sem.at[r])
        kept.start()
        started.append(kept)
        copies.append(started)

    upper = me >= lev_count // 2
    span = half_step * group
    width = place_ref.shape[1]
    sub = iota((8, width), 0)
    order = jnp.where(upper, sub, (sub // 4) * 4 + 3 - sub % 4)
    spread_by = jnp.concatenate([place_ref[...], place_ref[...]], axis=0)
    for r in range(cycles):
        for copy in copies[r]:
            copy.wait()
        rows = [[] for _ in range(4)]
        for first in range(0, lev_count, 4):
            for j in range(2):
                at = slice(j * LANES, (j + 1) * LANES)
                low_half, high_half = [], []
                for level in (first, first + 2):
                    one, two = got_ref[r, level, :, at], got_ref[r, level + 1, :, at]
                    turned = pltpu.roll(jnp.where(half_lane, two, one), 64, 1)
                    low_half.append(jnp.where(half_lane, one, turned))
                    high_half.append(jnp.where(half_lane, turned, two))
                rows[2 * j].append(jnp.concatenate(low_half, axis=1))
                rows[2 * j + 1].append(jnp.concatenate(high_half, axis=1))
        high, low = split(jnp.concatenate([row for quads in rows for row in quads], axis=0))
        spread = jnp.dot(jnp.concatenate([high, low], axis=1), spread_by, preferred_element_type=jnp.float32)
        sets = lev_count // 4
        for q in range(4):
            total = spread[8 * sets * q : 8 * sets * q + 8]
            for i in range(1, sets):
                total = total + pltpu.roll(spread[8 * (sets * q + i) : 8 * (sets * q + i) + 8], 4 * fields * i, 1)
            total = jnp.take_along_axis(total, order, axis=0, mode="promise_in_bounds")
            begin = q * quarter * group
            size = min(quarter * group, span - begin)
            for k in range(8):
                s = (k % 2) * 4 + k // 2
                out_ref[r : r + 1, k * span + begin : k * span + begin + size] = total[s : s + 1, :size]


def local(spectral, legendre, slot_wave, cycle_len, lat_order):
    slot_count = spectral.shape[2]
    degrees = spectral.shape[3]
    half_cycles = legendre.shape[1]
    lev_count = lax.axis_size("lev")
    wave_count = lax.axis_size("wave")
    slots = slot_wave.shape[0]
    padded_len = (RMAX + 8 * lev_count - 1) // (8 * lev_count) * 8 * lev_count
    points_dev = padded_len // lev_count
    half_step = points_dev // 8
    parts = spectral.shape[0] * spectral.shape[1]
    fields = parts // 2
    cycles = lat_order.shape[0] // wave_count
    groups = (slot_count + LANES - 1) // LANES
    chunk = 64 if slot_count % 64 == 0 else BLOCK
    half_rows = 2 * lev_count
    counts = (half_step + 15) // 16
    low_at = (16 * counts + LANES - 1) // LANES * LANES

    quarter = (half_step + 3) // 4
    assert fields * quarter <= 64 and half_step <= LANES and lev_count % 4 == 0
    wide = 2 * LANES
    width = (quarter * fields * lev_count + LANES - 1) // LANES * LANES
    smem = pl.BlockSpec(memory_space=pltpu.SMEM)
    vmem = pl.BlockSpec(memory_space=pltpu.VMEM)
    hbm = pl.BlockSpec(memory_space=pl.ANY)
    return pl.pallas_call(
        functools.partial(kernel, half_step, chunk),
        out_shape=pltpu.VMEM((cycles, points_dev * lev_count * fields), jnp.float32),
        in_specs=[vmem, smem, smem, hbm, hbm],
        out_specs=vmem,
        scratch_shapes=[
            pltpu.VMEM((parts, slot_count, degrees), jnp.bfloat16),
            pltpu.VMEM((half_cycles, slot_count, degrees), jnp.bfloat16),
            pltpu.VMEM((groups * LANES, LANES), jnp.float32),
            pltpu.VMEM((2 * half_cycles, 8, LANES), jnp.float32),
            pltpu.VMEM((groups, wave_count, cycles, 8, LANES), jnp.float32),
            pltpu.VMEM((groups, wave_count, cycles, 8, LANES), jnp.float32),
            pltpu.VMEM((cycles, 2, half_rows, slots), jnp.float32),
            pltpu.VMEM((cycles, 8, slots), jnp.float32),
            pltpu.VMEM((cycles, 2, slots // LANES, low_at + 16 * counts, LANES), jnp.bfloat16),
            pltpu.VMEM((2 * LANES, width), jnp.bfloat16),
            pltpu.VMEM((cycles, lev_count, 8, wide), jnp.float32),
            pltpu.VMEM((cycles, lev_count, 8, wide), jnp.float32),
            pltpu.SemaphoreType.DMA((2, slot_count // chunk)),
            pltpu.SemaphoreType.DMA((groups,)),
            pltpu.SemaphoreType.DMA((groups, wave_count)),
            pltpu.SemaphoreType.DMA((groups, wave_count)),
            pltpu.SemaphoreType.DMA((cycles,)),
            pltpu.SemaphoreType.DMA((cycles, lev_count)),
            pltpu.SemaphoreType.DMA((cycles, lev_count)),
        ],
        compiler_params=pltpu.CompilerParams(collective_id=0, has_side_effects=True),
        name="transform",
    )(
        slot_wave, lat_order, cycle_len,
        spectral.reshape(parts, slot_count, degrees), jnp.transpose(legendre, (1, 0, 2)),
    )


def solution(mesh):
    in_specs = (P("lev", None, "wave", None), P("wave", None, None), P(), P(), P())
    out_specs = P("wave", "lev")
    return jax.shard_map(local, mesh=mesh, in_specs=in_specs, out_specs=out_specs, check_vma=False)
```

```python
import functools
import math

import jax
import jax.numpy as jnp
from jax import lax
from jax.experimental import pallas as pl
from jax.experimental.pallas import tpu as pltpu
from jax.sharding import PartitionSpec as P

RMAX = 5136
LANES = 128
BLOCK = 16
AHEAD = 3


def split(value):
    high = value.astype(jnp.bfloat16)
    return high, (value - high.astype(jnp.float32)).astype(jnp.bfloat16)


def dot_nt(left, right):
    return lax.dot_general(left, right, (((1,), (1,)), ((), ())), preferred_element_type=jnp.float32)


def turns(t):
    y = math.pi * t
    z = y * y
    sine = jnp.full_like(z, 1.0 / math.factorial(13))
    for n in (11, 9, 7, 5, 3, 1):
        sign = -1.0 if (n // 2) % 2 else 1.0
        sine = sine * z + sign / math.factorial(n)
    sine = sine * y
    cosine = jnp.full_like(z, 1.0 / math.factorial(12))
    for n in (10, 8, 6, 4, 2, 0):
        sign = -1.0 if (n // 2) % 2 else 1.0
        cosine = cosine * z + sign / math.factorial(n)
    return 1.0 - 2.0 * sine * sine, 2.0 * sine * cosine


def iota(shape, dim):
    return lax.broadcasted_iota(jnp.int32, shape, dim)


def kernel(
    half_step, chunks,
    wave_hbm, lat_hbm, cycle_hbm, spec_hbm, leg_hbm, out_ref,
    wave_ref, lat_ref, cycle_ref,
    spec_ref, leg_ref, col_ref, four_ref, wsend_ref, wgot_ref,
    twist_ref, cen_ref, tab_ref, place_ref, send_ref, got_ref,
    small_sem, load_sem, wown_sem, wsend_sem, wrecv_sem, own_sem, send_sem, recv_sem,
):
    parts, slot_count, degrees = spec_ref.shape
    half_cycles = leg_ref.shape[0]
    fields = parts // 2
    groups, wave_count, cycles = wsend_ref.shape[:3]
    lev_count = send_ref.shape[1]
    wide = send_ref.shape[-1]
    slots = wave_ref.shape[0]
    tiles = slots // LANES
    step = 2 * half_step
    points_dev = 4 * step
    half_rows = twist_ref.shape[2]
    blocks = half_rows // 8
    counts = (half_step + 15) // 16
    low_at = tab_ref.shape[3] - 16 * counts
    me = lax.axis_index("lev")
    my_wave = lax.axis_index("wave")
    first_row = my_wave * cycles

    loads, starts = [], []
    start = 0
    for i, size in enumerate(chunks):
        at = pl.ds(start, size)
        loads.append([
            pltpu.make_async_copy(leg_hbm.at[:, at], leg_ref.at[:, at], load_sem.at[0, i]),
            pltpu.make_async_copy(spec_hbm.at[:, at], spec_ref.at[:, at], load_sem.at[1, i]),
        ])
        starts.append(start)
        start += size
    small = [
        pltpu.make_async_copy(source, target, small_sem.at[i])
        for i, (source, target) in enumerate(((wave_hbm, wave_ref), (lat_hbm, lat_ref), (cycle_hbm, cycle_ref)))
    ]
    for copy in small:
        copy.start()
    for pair in loads[:AHEAD]:
        for copy in pair:
            copy.start()
    barrier = pltpu.get_barrier_semaphore()
    for offset in range(1, lev_count):
        peer = lax.rem(me + offset, lev_count)
        pl.semaphore_signal(barrier, inc=1, device_id={"lev": peer}, device_id_type=pl.DeviceIdType.MESH)
    for offset in range(1, wave_count):
        peer = lax.rem(my_wave + offset, wave_count)
        pl.semaphore_signal(barrier, inc=1, device_id={"wave": peer}, device_id_type=pl.DeviceIdType.MESH)
    for copy in small:
        copy.wait()

    waves = wave_ref[...].reshape(1, slots).astype(jnp.float32)

    mine = pltpu.roll(waves, slots - my_wave * slot_count, 1)
    eye = iota((LANES, LANES), 0) == iota((LANES, LANES), 1)
    for g in range(groups):
        column = jnp.sum(jnp.where(eye, mine[:, g * LANES : (g + 1) * LANES], 0.0), axis=1, keepdims=True)
        col_ref[g * LANES : (g + 1) * LANES] = column - iota((LANES, LANES), 1).astype(jnp.float32)

    near = [i + 0.5 for i in range(8)]
    twist = [step * (i + 0.5) for i in range(8)]
    rest = [16.0 * k + 8.0 for k in range(counts)] + [8.0 * step * a for a in range(1, blocks)]
    rest += [(lev_count * points_dev - 1) / 2]
    rest_count = len(rest)
    rest_rows = (rest_count + 7) // 8 * 8
    row = iota((rest_rows, 1), 0)
    row8 = iota((8, 1), 0).astype(jnp.float32) + 0.5
    rest_mult = jnp.zeros((rest_rows, 1), jnp.float32)
    for i, value in enumerate(rest):
        rest_mult = jnp.where(row == i, value, rest_mult)
    mult = jnp.concatenate([row8, row8 * step, rest_mult], axis=0)
    lengths = [
        cycle_ref[lat_ref[first_row + r] % half_cycles].astype(jnp.float32) for r in range(cycles)
    ]
    if low_at > 16 * counts:
        hole = low_at - 16 * counts
        tab_ref[:, :, :, 16 * counts : low_at, :] = jnp.zeros((cycles, 2, tiles, hole, LANES), jnp.bfloat16)

    def tables(r, t):
        at = slice(t * LANES, (t + 1) * LANES)
        wave = waves[:, at]
        length = lengths[r]
        inverse = 1.0 / jnp.full((1, LANES), length)
        phase = wave * mult
        whole = jnp.floor(phase * inverse + 0.5)
        cosine, sine = turns((phase - whole * length) * inverse)
        nc, ns, tc, ts = cosine[0:8], sine[0:8], cosine[8:16], sine[8:16]
        rc, rs = cosine[16:], sine[16:]
        twist_ref[r, 0, 0:8, at] = tc
        twist_ref[r, 1, 0:8, at] = ts
        for a in range(1, blocks):
            i = counts + a - 1
            c, s = rc[i : i + 1], rs[i : i + 1]
            twist_ref[r, 0, 8 * a : 8 * a + 8, at] = tc * c - ts * s
            twist_ref[r, 1, 8 * a : 8 * a + 8, at] = ts * c + tc * s
        weight = jnp.where(wave == 0.0, 1.0, 2.0)
        i = rest_count - 1
        cen_ref[r, 0:1, at] = rc[i : i + 1] * weight
        cen_ref[r, 1:2, at] = rs[i : i + 1] * weight
        for k in range(counts):
            c, s = rc[k : k + 1], rs[k : k + 1]
            cc, ss, sc, cs = c * nc, s * ns, s * nc, c * ns
            for which, value in (
                (0, jnp.concatenate([cc + ss, cc - ss], axis=0)),
                (1, jnp.concatenate([sc - cs, sc + cs], axis=0)),
            ):
                high, low = split(value)
                tab_ref[r, which, t, 16 * k : 16 * k + 16, :] = high
                tab_ref[r, which, t, low_at + 16 * k : low_at + 16 * k + 16, :] = low

    turns_count = LANES // BLOCK
    lane = iota((1, LANES), 1)
    lane_chunk = lane // BLOCK
    flip = jnp.where((iota((BLOCK, LANES), 1) & 1) == 1, -1.0, 1.0).astype(jnp.bfloat16)
    lats = 2 * half_cycles
    own = iota((BLOCK, lats * BLOCK), 0) == iota((BLOCK, lats * BLOCK), 1) % BLOCK

    def legendre(b, turn):
        at = slice(b * BLOCK, (b + 1) * BLOCK)
        column = col_ref[at, :]
        order = [(j - turn) % lats for j in range(lats)]
        columns = []
        for d in range(0, degrees, LANES):
            live = jnp.where(column <= float(d), 1.0, 0.0).astype(jnp.bfloat16)
            north = [live * leg_ref[k, at, d : d + LANES] for k in range(half_cycles)]
            both = north + [flip * value for value in north]
            columns.append(jnp.concatenate([both[j] for j in order], axis=0))
        table = jnp.concatenate(columns, axis=1)
        product = dot_nt(spec_ref[:, at, :].reshape(parts * BLOCK, degrees), table)
        product = product.reshape(parts, BLOCK, lats * BLOCK)
        total = jnp.sum(jnp.where(own[None], product, 0.0), axis=1)
        extra = -total.shape[1] % LANES
        if extra:
            total = jnp.concatenate([total, jnp.zeros((parts, extra), jnp.float32)], axis=1)
        return [total[:, j * LANES : (j + 1) * LANES] for j in range(total.shape[1] // LANES)]

    wave_copies = []

    def send_group(g, sums):
        sign = jnp.where((mine[:, g * LANES : (g + 1) * LANES].astype(jnp.int32) & 1) == 1, -1.0, 1.0)
        for j in range(lats):
            shifts = {}
            for b, total in enumerate(sums):
                place = (j + b) % lats
                shifts.setdefault((b - place) % turns_count, []).append(
                    (b, place % turns_count, total[place // turns_count])
                )
            value = None
            for shift, members in shifts.items():
                picked = None
                for b, at_chunk, total in members:
                    picked = total if picked is None else jnp.where(lane_chunk == at_chunk, total, picked)
                if shift:
                    picked = pltpu.roll(picked, shift * BLOCK, 1)
                first, last = members[0][0], members[-1][0]
                if value is None:
                    value = picked
                else:
                    value = jnp.where((lane_chunk >= first) & (lane_chunk <= last), picked, value)
            if j >= half_cycles:
                value = value * sign
            four_ref[j, 0:parts, :] = value
        for w in range(wave_count):
            for r in range(cycles):
                wsend_ref[g, w, r] = four_ref[lat_ref[w * cycles + r]]
        if g == 0:
            pl.semaphore_wait(barrier, lev_count + wave_count - 2)
        for offset in range(1, wave_count):
            peer = lax.rem(my_wave + offset, wave_count)
            copy = pltpu.make_async_remote_copy(
                src_ref=wsend_ref.at[g, peer],
                dst_ref=wgot_ref.at[g, my_wave],
                send_sem=wsend_sem.at[g, offset],
                recv_sem=wrecv_sem.at[g, offset],
                device_id={"wave": peer},
                device_id_type=pl.DeviceIdType.MESH,
            )
            copy.start()
            wave_copies.append(copy)
        kept = pltpu.make_async_copy(wsend_ref.at[g, my_wave], wgot_ref.at[g, my_wave], wown_sem.at[g])
        kept.start()
        wave_copies.append(kept)

    for t in range(tiles):
        tables(0, t)
    total_blocks = slot_count // BLOCK
    sums = []
    for b in range(total_blocks):
        if b * BLOCK in starts:
            i = starts.index(b * BLOCK)
            for copy in loads[i]:
                copy.wait()
            for copy in loads[i + AHEAD] if i + AHEAD < len(loads) else ():
                copy.start()
        sums.append(legendre(b, b % turns_count))
        if b % turns_count == turns_count - 1 or b == total_blocks - 1:
            send_group(b // turns_count, sums)
            sums = []
    for t in range(tiles if cycles > 1 else 0):
        tables(1, t)

    group = lev_count * fields
    quarter = (half_step + 3) // 4
    source = iota((4 * 64, 1), 0)
    inner = source % 64
    target = jnp.where(
        inner < fields * quarter, (inner % quarter) * group + source // 64 * fields + inner // quarter, -1
    )
    for j in range(place_ref.shape[1] // LANES):
        at = slice(j * LANES, (j + 1) * LANES)
        place_ref[:, at] = jnp.where(iota((4 * 64, LANES), 1) + j * LANES == target, 1.0, 0.0).astype(jnp.bfloat16)

    picks = {}
    inner = lane % 64
    for j in range(2):
        for f in range(fields):
            point = inner - f * quarter
            point = (2 * j + lane // 64) * quarter + jnp.clip(point, 0, quarter - 1)
            for back in (0, 1):
                p = half_step - 1 - point if back else point
                p = jnp.clip(p, 0, half_step - 1)
                low = p % 16
                index = p - low + jnp.where(low < 8, 7 - low, low)
                picks[j, f, back] = jnp.broadcast_to(index, (half_rows, LANES))
    where_lane = iota((8, wide), 1)
    where_row = iota((8, wide), 0)
    inner = where_lane % 64
    inside = where_lane // 64 * quarter + inner % quarter
    inside = jnp.where((inner < fields * quarter) & (inside < half_step), inside, 1 << 20)
    reach = {}
    for upper in (0, 1):
        i = where_row % 4 if upper else 3 - where_row % 4
        reach[upper] = (step * i + half_step * (where_row // 4) + inside).astype(jnp.float32)
    half_lane = lane < 64

    for copy in wave_copies:
        copy.wait()

    copies = []
    odd_row = iota((8, 1), 0) % 2
    turn_sign = jnp.where(odd_row == 1, 1.0, -1.0)
    for r in range(cycles):
        for t in range(tiles if r > 1 else 0):
            tables(r, t)
        operands = ([], [])
        for t in range(tiles):
            at = slice(t * LANES, (t + 1) * LANES)
            coef = None
            position = t * LANES
            while position < (t + 1) * LANES:
                w, inner = position // slot_count, position % slot_count
                g, start = inner // LANES, inner % LANES
                size = min((t + 1) * LANES - position, slot_count - inner, LANES - start)
                piece = wgot_ref[g, w, r]
                to = position - t * LANES
                if to != start:
                    piece = pltpu.roll(piece, (to - start) % LANES, 1)
                coef = piece if coef is None else jnp.where(lane >= to, piece, coef)
                position += size
            swapped = jnp.where(odd_row == 1, pltpu.roll(coef, 1, 0), pltpu.roll(coef, 7, 0))
            coef = coef * cen_ref[r, 0:1, at] + swapped * (cen_ref[r, 1:2, at] * turn_sign)
            tc, ts = twist_ref[r, 0, :, at], twist_ref[r, 1, :, at]
            pairs = ([], [])
            for first in (0, 1):
                for f in range(fields):
                    part = coef[2 * f + first : 2 * f + first + 1]
                    for which in (0, 1):
                        pairs[which].append(split(part * (tc if which == first else ts)))
            for which in (0, 1):
                operands[which].append(
                    jnp.concatenate([high for high, _ in pairs[which]] + [low for _, low in pairs[which]], axis=0)
                )
        both = []
        rows = 2 * fields * half_rows
        for which in (0, 1):
            table = jnp.concatenate([tab_ref[r, which, t] for t in range(tiles)], axis=1)
            product = dot_nt(jnp.concatenate(operands[which], axis=1), table)
            value = product[:rows] + product[rows:]
            both.append(value[:, :LANES] + jnp.concatenate([value[:, low_at:], jnp.zeros((rows, low_at - 16 * counts), jnp.float32)], axis=1))
        mixed = {}
        for f in range(fields):
            p1, p2 = (both[0][(i * fields + f) * half_rows : (i * fields + f + 1) * half_rows] for i in (0, 1))
            p3, p4 = (both[1][(i * fields + f) * half_rows : (i * fields + f + 1) * half_rows] for i in (0, 1))
            for upper, even, odd in ((1, p1 - p2, p3 + p4), (0, p1 + p2, p4 - p3)):
                for back, value in ((0, even - odd), (1, even + odd)):
                    for j in range(2):
                        mixed[upper, back, j, f] = jnp.take_along_axis(
                            value, picks[j, f, back], axis=1, mode="promise_in_bounds"
                        )
        inner = lane % 64
        for upper in (0, 1):
            row_tiles = []
            for back in (1, 0):
                pieces = []
                for j in range(2):
                    piece = mixed[upper, back, j, 0]
                    for f in range(1, fields):
                        piece = jnp.where(inner >= f * quarter, mixed[upper, back, j, f], piece)
                    pieces.append(piece)
                row_tiles.append(jnp.concatenate(pieces, axis=1))
            for a in range(lev_count // 2):
                dest = lev_count // 2 + a if upper else lev_count // 2 - 1 - a
                tile = jnp.concatenate([value[4 * a : 4 * a + 4] for value in row_tiles], axis=0)
                send_ref[r, dest] = jnp.where(reach[upper] < lengths[r] - float(points_dev * dest), tile, 0.0)
        started = []
        paired = lev_count & (lev_count - 1) == 0
        for offset in range(lev_count - 1, 0, -1):
            peer = me ^ offset if paired else lax.rem(me + offset, lev_count)
            copy = pltpu.make_async_remote_copy(
                src_ref=send_ref.at[r, peer],
                dst_ref=got_ref.at[r, me],
                send_sem=send_sem.at[r, offset],
                recv_sem=recv_sem.at[r, offset],
                device_id={"lev": peer},
                device_id_type=pl.DeviceIdType.MESH,
            )
            copy.start()
            started.append(copy)
        kept = pltpu.make_async_copy(send_ref.at[r, me], got_ref.at[r, me], own_sem.at[r])
        kept.start()
        started.append(kept)
        copies.append(started)

    upper = me >= lev_count // 2
    span = half_step * group
    width = place_ref.shape[1]
    sub = iota((8, width), 0)
    order = jnp.where(upper, sub, (sub // 4) * 4 + 3 - sub % 4)
    spread_by = jnp.concatenate([place_ref[...], place_ref[...]], axis=0)
    for r in range(cycles):
        for copy in copies[r]:
            copy.wait()
        rows = [[] for _ in range(4)]
        for first in range(0, lev_count, 4):
            for j in range(2):
                at = slice(j * LANES, (j + 1) * LANES)
                low_half, high_half = [], []
                for level in (first, first + 2):
                    one, two = got_ref[r, level, :, at], got_ref[r, level + 1, :, at]
                    turned = pltpu.roll(jnp.where(half_lane, two, one), 64, 1)
                    low_half.append(jnp.where(half_lane, one, turned))
                    high_half.append(jnp.where(half_lane, turned, two))
                rows[2 * j].append(jnp.concatenate(low_half, axis=1))
                rows[2 * j + 1].append(jnp.concatenate(high_half, axis=1))
        high, low = split(jnp.concatenate([row for quads in rows for row in quads], axis=0))
        spread = jnp.dot(jnp.concatenate([high, low], axis=1), spread_by, preferred_element_type=jnp.float32)
        sets = lev_count // 4
        for q in range(4):
            total = spread[8 * sets * q : 8 * sets * q + 8]
            for i in range(1, sets):
                total = total + pltpu.roll(spread[8 * (sets * q + i) : 8 * (sets * q + i) + 8], 4 * fields * i, 1)
            total = jnp.take_along_axis(total, order, axis=0, mode="promise_in_bounds")
            begin = q * quarter * group
            size = min(quarter * group, span - begin)
            for k in range(8):
                s = (k % 2) * 4 + k // 2
                out_ref[r : r + 1, k * span + begin : k * span + begin + size] = total[s : s + 1, :size]


def local(spectral, legendre, slot_wave, cycle_len, lat_order):
    slot_count = spectral.shape[2]
    degrees = spectral.shape[3]
    half_cycles = legendre.shape[1]
    lev_count = lax.axis_size("lev")
    wave_count = lax.axis_size("wave")
    slots = slot_wave.shape[0]
    padded_len = (RMAX + 8 * lev_count - 1) // (8 * lev_count) * 8 * lev_count
    points_dev = padded_len // lev_count
    half_step = points_dev // 8
    parts = spectral.shape[0] * spectral.shape[1]
    fields = parts // 2
    cycles = lat_order.shape[0] // wave_count
    groups = (slot_count + LANES - 1) // LANES
    chunks, left = [], slot_count
    while left:
        size = 64 if left > 64 else min(left, 32)
        chunks.append(size)
        left -= size
    half_rows = 2 * lev_count
    counts = (half_step + 15) // 16
    low_at = (16 * counts + LANES - 1) // LANES * LANES

    quarter = (half_step + 3) // 4
    assert fields * quarter <= 64 and half_step <= LANES and lev_count % 4 == 0
    wide = 2 * LANES
    width = (quarter * fields * lev_count + LANES - 1) // LANES * LANES
    vmem = pl.BlockSpec(memory_space=pltpu.VMEM)
    hbm = pl.BlockSpec(memory_space=pl.ANY)
    return pl.pallas_call(
        functools.partial(kernel, half_step, tuple(chunks)),
        out_shape=pltpu.VMEM((cycles, points_dev * lev_count * fields), jnp.float32),
        in_specs=[hbm] * 5,
        out_specs=vmem,
        scratch_shapes=[
            pltpu.VMEM(slot_wave.shape, jnp.int32),
            pltpu.SMEM(lat_order.shape, jnp.int32),
            pltpu.SMEM(cycle_len.shape, jnp.int32),
            pltpu.VMEM((parts, slot_count, degrees), jnp.bfloat16),
            pltpu.VMEM((half_cycles, slot_count, degrees), jnp.bfloat16),
            pltpu.VMEM((groups * LANES, LANES), jnp.float32),
            pltpu.VMEM((2 * half_cycles, 8, LANES), jnp.float32),
            pltpu.VMEM((groups, wave_count, cycles, 8, LANES), jnp.float32),
            pltpu.VMEM((groups, wave_count, cycles, 8, LANES), jnp.float32),
            pltpu.VMEM((cycles, 2, half_rows, slots), jnp.float32),
            pltpu.VMEM((cycles, 8, slots), jnp.float32),
            pltpu.VMEM((cycles, 2, slots // LANES, low_at + 16 * counts, LANES), jnp.bfloat16),
            pltpu.VMEM((2 * LANES, width), jnp.bfloat16),
            pltpu.VMEM((cycles, lev_count, 8, wide), jnp.float32),
            pltpu.VMEM((cycles, lev_count, 8, wide), jnp.float32),
            pltpu.SemaphoreType.DMA((3,)),
            pltpu.SemaphoreType.DMA((2, len(chunks))),
            pltpu.SemaphoreType.DMA((groups,)),
            pltpu.SemaphoreType.DMA((groups, wave_count)),
            pltpu.SemaphoreType.DMA((groups, wave_count)),
            pltpu.SemaphoreType.DMA((cycles,)),
            pltpu.SemaphoreType.DMA((cycles, lev_count)),
            pltpu.SemaphoreType.DMA((cycles, lev_count)),
        ],
        compiler_params=pltpu.CompilerParams(collective_id=0, has_side_effects=True),
        name="transform",
    )(
        slot_wave, lat_order, cycle_len,
        spectral.reshape(parts, slot_count, degrees), jnp.transpose(legendre, (1, 0, 2)),
    )


def solution(mesh):
    in_specs = (P("lev", None, "wave", None), P("wave", None, None), P(), P(), P())
    out_specs = P("wave", "lev")
    return jax.shard_map(local, mesh=mesh, in_specs=in_specs, out_specs=out_specs, check_vma=False)
```

```python
import functools
import math

import jax
import jax.numpy as jnp
from jax import lax
from jax.experimental import pallas as pl
from jax.experimental.pallas import tpu as pltpu
from jax.sharding import PartitionSpec as P

RMAX = 5136
LANES = 128
BLOCK = 16
AHEAD = 3


def split(value):
    high = value.astype(jnp.bfloat16)
    return high, (value - high.astype(jnp.float32)).astype(jnp.bfloat16)


def dot_nt(left, right):
    return lax.dot_general(left, right, (((1,), (1,)), ((), ())), preferred_element_type=jnp.float32)


def turns(t):
    y = math.pi * t
    z = y * y
    sine = jnp.full_like(z, 1.0 / math.factorial(13))
    for n in (11, 9, 7, 5, 3, 1):
        sign = -1.0 if (n // 2) % 2 else 1.0
        sine = sine * z + sign / math.factorial(n)
    sine = sine * y
    cosine = jnp.full_like(z, 1.0 / math.factorial(12))
    for n in (10, 8, 6, 4, 2, 0):
        sign = -1.0 if (n // 2) % 2 else 1.0
        cosine = cosine * z + sign / math.factorial(n)
    return 1.0 - 2.0 * sine * sine, 2.0 * sine * cosine


def iota(shape, dim):
    return lax.broadcasted_iota(jnp.int32, shape, dim)


def kernel(
    half_step, chunks,
    wave_hbm, lat_hbm, cycle_hbm, spec_hbm, leg_hbm, out_ref,
    wave_ref, lat_ref, cycle_ref,
    spec_ref, leg_ref, col_ref, four_ref, wsend_ref, wgot_ref,
    twist_ref, cen_ref, tab_ref, place_ref, send_ref, got_ref,
    small_sem, load_sem, wown_sem, wsend_sem, wrecv_sem, own_sem, send_sem, recv_sem,
):
    parts, slot_count, degrees = spec_ref.shape
    half_cycles = leg_ref.shape[0]
    fields = parts // 2
    groups, wave_count, cycles = wsend_ref.shape[:3]
    lev_count = send_ref.shape[1]
    wide = send_ref.shape[-1]
    slots = wave_ref.shape[0]
    tiles = slots // LANES
    step = 2 * half_step
    points_dev = 4 * step
    half_rows = twist_ref.shape[2]
    blocks = half_rows // 8
    counts = (half_step + 15) // 16
    low_at = tab_ref.shape[3] - 16 * counts
    me = lax.axis_index("lev")
    my_wave = lax.axis_index("wave")
    first_row = my_wave * cycles

    loads, starts = [], []
    start = 0
    for i, size in enumerate(chunks):
        at = pl.ds(start, size)
        loads.append([
            pltpu.make_async_copy(leg_hbm.at[:, at], leg_ref.at[:, at], load_sem.at[0, i]),
            pltpu.make_async_copy(spec_hbm.at[:, at], spec_ref.at[:, at], load_sem.at[1, i]),
        ])
        starts.append(start)
        start += size
    small = [
        pltpu.make_async_copy(source, target, small_sem.at[i])
        for i, (source, target) in enumerate(((wave_hbm, wave_ref), (lat_hbm, lat_ref), (cycle_hbm, cycle_ref)))
    ]
    for copy in small:
        copy.start()
    for pair in loads[:AHEAD]:
        for copy in pair:
            copy.start()
    barrier = pltpu.get_barrier_semaphore()
    for offset in range(1, lev_count):
        peer = lax.rem(me + offset, lev_count)
        pl.semaphore_signal(barrier, inc=1, device_id={"lev": peer}, device_id_type=pl.DeviceIdType.MESH)
    for offset in range(1, wave_count):
        peer = lax.rem(my_wave + offset, wave_count)
        pl.semaphore_signal(barrier, inc=1, device_id={"wave": peer}, device_id_type=pl.DeviceIdType.MESH)
    for copy in small:
        copy.wait()

    waves = wave_ref[...].reshape(1, slots).astype(jnp.float32)

    mine = pltpu.roll(waves, slots - my_wave * slot_count, 1)
    eye = iota((LANES, LANES), 0) == iota((LANES, LANES), 1)
    for g in range(groups):
        column = jnp.sum(jnp.where(eye, mine[:, g * LANES : (g + 1) * LANES], 0.0), axis=1, keepdims=True)
        col_ref[g * LANES : (g + 1) * LANES] = column - iota((LANES, LANES), 1).astype(jnp.float32)

    near = [i + 0.5 for i in range(8)]
    twist = [step * (i + 0.5) for i in range(8)]
    rest = [16.0 * k + 8.0 for k in range(counts)] + [8.0 * step * a for a in range(1, blocks)]
    rest += [(lev_count * points_dev - 1) / 2]
    rest_count = len(rest)
    rest_rows = (rest_count + 7) // 8 * 8
    row = iota((rest_rows, 1), 0)
    row8 = iota((8, 1), 0).astype(jnp.float32) + 0.5
    rest_mult = jnp.zeros((rest_rows, 1), jnp.float32)
    for i, value in enumerate(rest):
        rest_mult = jnp.where(row == i, value, rest_mult)
    mult = jnp.concatenate([row8, row8 * step, rest_mult], axis=0)
    lengths = [
        cycle_ref[lat_ref[first_row + r] % half_cycles].astype(jnp.float32) for r in range(cycles)
    ]
    if low_at > 16 * counts:
        hole = low_at - 16 * counts
        tab_ref[:, :, :, 16 * counts : low_at, :] = jnp.zeros((cycles, 2, tiles, hole, LANES), jnp.bfloat16)

    def tables(r, t):
        at = slice(t * LANES, (t + 1) * LANES)
        wave = waves[:, at]
        length = lengths[r]
        inverse = 1.0 / jnp.full((1, LANES), length)
        phase = wave * mult
        whole = jnp.floor(phase * inverse + 0.5)
        cosine, sine = turns((phase - whole * length) * inverse)
        nc, ns, tc, ts = cosine[0:8], sine[0:8], cosine[8:16], sine[8:16]
        rc, rs = cosine[16:], sine[16:]
        twist_ref[r, 0, 0:8, at] = tc
        twist_ref[r, 1, 0:8, at] = ts
        for a in range(1, blocks):
            i = counts + a - 1
            c, s = rc[i : i + 1], rs[i : i + 1]
            twist_ref[r, 0, 8 * a : 8 * a + 8, at] = tc * c - ts * s
            twist_ref[r, 1, 8 * a : 8 * a + 8, at] = ts * c + tc * s
        weight = jnp.where(wave == 0.0, 1.0, 2.0)
        i = rest_count - 1
        cen_ref[r, 0:1, at] = rc[i : i + 1] * weight
        cen_ref[r, 1:2, at] = rs[i : i + 1] * weight
        for k in range(counts):
            c, s = rc[k : k + 1], rs[k : k + 1]
            cc, ss, sc, cs = c * nc, s * ns, s * nc, c * ns
            for which, value in (
                (0, jnp.concatenate([cc + ss, cc - ss], axis=0)),
                (1, jnp.concatenate([sc - cs, sc + cs], axis=0)),
            ):
                high, low = split(value)
                tab_ref[r, which, t, 16 * k : 16 * k + 16, :] = high
                tab_ref[r, which, t, low_at + 16 * k : low_at + 16 * k + 16, :] = low

    turns_count = LANES // BLOCK
    lane = iota((1, LANES), 1)
    lane_chunk = lane // BLOCK
    flip = jnp.where((iota((BLOCK, LANES), 1) & 1) == 1, -1.0, 1.0).astype(jnp.bfloat16)
    lats = 2 * half_cycles
    own = iota((BLOCK, parts * BLOCK), 0) == iota((BLOCK, parts * BLOCK), 1) % BLOCK
    south_row = iota((lats, 1), 0) >= half_cycles

    def legendre(b):
        at = slice(b * BLOCK, (b + 1) * BLOCK)
        column = col_ref[at, :]
        columns = []
        for d in range(0, degrees, LANES):
            live = jnp.where(column <= float(d), 1.0, 0.0).astype(jnp.bfloat16)
            north = [live * leg_ref[k, at, d : d + LANES] for k in range(half_cycles)]
            columns.append(jnp.concatenate(north + [flip * value for value in north], axis=0))
        rows = jnp.concatenate([spec_ref[(j - b) % parts, at, :] for j in range(parts)], axis=0)
        return dot_nt(jnp.concatenate(columns, axis=1), rows)

    def diagonal(product):
        product = product.reshape(lats, BLOCK, parts * BLOCK)
        total = jnp.sum(jnp.where(own[None], product, 0.0), axis=1)
        return jnp.concatenate([total, jnp.zeros((lats, LANES - parts * BLOCK), jnp.float32)], axis=1)

    wave_copies = []

    def send_group(g, sums):
        odd = (mine[:, g * LANES : (g + 1) * LANES].astype(jnp.int32) & 1) == 1
        sign = jnp.where(south_row & odd, -1.0, 1.0)
        for c in range(parts):
            shifts = {}
            for i, (b, total) in enumerate(sums):
                place = (c + b) % parts
                shifts.setdefault((i - place) % turns_count, []).append((i, place, total))
            value = None
            for shift, members in shifts.items():
                picked = None
                for i, place, total in members:
                    picked = total if picked is None else jnp.where(lane_chunk == place, total, picked)
                if shift:
                    picked = pltpu.roll(picked, shift * BLOCK, 1)
                if value is None:
                    value = picked
                else:
                    mask = lane_chunk == members[0][0]
                    for i, _, _ in members[1:]:
                        mask = mask | (lane_chunk == i)
                    value = jnp.where(mask, picked, value)
            four_ref[:, c, :] = value * sign
        for w in range(wave_count):
            for r in range(cycles):
                wsend_ref[g, w, r] = four_ref[lat_ref[w * cycles + r]]
        if g == 0:
            pl.semaphore_wait(barrier, lev_count + wave_count - 2)
        for offset in range(1, wave_count):
            peer = lax.rem(my_wave + offset, wave_count)
            copy = pltpu.make_async_remote_copy(
                src_ref=wsend_ref.at[g, peer],
                dst_ref=wgot_ref.at[g, my_wave],
                send_sem=wsend_sem.at[g, offset],
                recv_sem=wrecv_sem.at[g, offset],
                device_id={"wave": peer},
                device_id_type=pl.DeviceIdType.MESH,
            )
            copy.start()
            wave_copies.append(copy)
        kept = pltpu.make_async_copy(wsend_ref.at[g, my_wave], wgot_ref.at[g, my_wave], wown_sem.at[g])
        kept.start()
        wave_copies.append(kept)

    early = min(2, cycles)
    for r in range(early):
        for t in range(tiles):
            tables(r, t)
    total_blocks = slot_count // BLOCK
    sums = []

    def finish(b, product):
        sums.append((b, diagonal(product)))
        if b % turns_count == turns_count - 1 or b == total_blocks - 1:
            send_group(b // turns_count, sums)
            sums.clear()

    pending = None
    for b in range(total_blocks):
        if b * BLOCK in starts:
            i = starts.index(b * BLOCK)
            for copy in loads[i]:
                copy.wait()
            for copy in loads[i + AHEAD] if i + AHEAD < len(loads) else ():
                copy.start()
        product = legendre(b)
        if pending is not None:
            finish(*pending)
        pending = (b, product)
    finish(*pending)
    for r in range(early, cycles):
        for t in range(tiles):
            tables(r, t)

    group = lev_count * fields
    quarter = (half_step + 3) // 4
    source = iota((4 * 64, 1), 0)
    inner = source % 64
    target = jnp.where(
        inner < fields * quarter, (inner % quarter) * group + source // 64 * fields + inner // quarter, -1
    )
    for j in range(place_ref.shape[1] // LANES):
        at = slice(j * LANES, (j + 1) * LANES)
        place_ref[:, at] = jnp.where(iota((4 * 64, LANES), 1) + j * LANES == target, 1.0, 0.0).astype(jnp.bfloat16)

    picks = {}
    inner = lane % 64
    for j in range(2):
        for f in range(fields):
            point = inner - f * quarter
            point = (2 * j + lane // 64) * quarter + jnp.clip(point, 0, quarter - 1)
            for back in (0, 1):
                p = half_step - 1 - point if back else point
                p = jnp.clip(p, 0, half_step - 1)
                low = p % 16
                index = p - low + jnp.where(low < 8, 7 - low, low)
                picks[j, f, back] = jnp.broadcast_to(index, (half_rows, LANES))
    where_lane = iota((8, wide), 1)
    where_row = iota((8, wide), 0)
    inner = where_lane % 64
    inside = where_lane // 64 * quarter + inner % quarter
    inside = jnp.where((inner < fields * quarter) & (inside < half_step), inside, 1 << 20)
    reach = {}
    for upper in (0, 1):
        i = where_row % 4 if upper else 3 - where_row % 4
        reach[upper] = (step * i + half_step * (where_row // 4) + inside).astype(jnp.float32)
    half_lane = lane < 64

    for copy in wave_copies:
        copy.wait()

    copies = []
    odd_row = iota((8, 1), 0) % 2
    turn_sign = jnp.where(odd_row == 1, 1.0, -1.0)
    for r in range(cycles):
        operands = ([], [])
        for t in range(tiles):
            at = slice(t * LANES, (t + 1) * LANES)
            coef = None
            position = t * LANES
            while position < (t + 1) * LANES:
                w, inner = position // slot_count, position % slot_count
                g, start = inner // LANES, inner % LANES
                size = min((t + 1) * LANES - position, slot_count - inner, LANES - start)
                piece = wgot_ref[g, w, r]
                to = position - t * LANES
                if to != start:
                    piece = pltpu.roll(piece, (to - start) % LANES, 1)
                coef = piece if coef is None else jnp.where(lane >= to, piece, coef)
                position += size
            swapped = jnp.where(odd_row == 1, pltpu.roll(coef, 1, 0), pltpu.roll(coef, 7, 0))
            coef = coef * cen_ref[r, 0:1, at] + swapped * (cen_ref[r, 1:2, at] * turn_sign)
            tc, ts = twist_ref[r, 0, :, at], twist_ref[r, 1, :, at]
            pairs = ([], [])
            for first in (0, 1):
                for f in range(fields):
                    part = coef[2 * f + first : 2 * f + first + 1]
                    for which in (0, 1):
                        pairs[which].append(split(part * (tc if which == first else ts)))
            for which in (0, 1):
                operands[which].append(
                    jnp.concatenate([high for high, _ in pairs[which]] + [low for _, low in pairs[which]], axis=0)
                )
        both = []
        rows = 2 * fields * half_rows
        for which in (0, 1):
            table = jnp.concatenate([tab_ref[r, which, t] for t in range(tiles)], axis=1)
            product = dot_nt(jnp.concatenate(operands[which], axis=1), table)
            value = product[:rows] + product[rows:]
            both.append(value[:, :LANES] + jnp.concatenate([value[:, low_at:], jnp.zeros((rows, low_at - 16 * counts), jnp.float32)], axis=1))
        mixed = {}
        for f in range(fields):
            p1, p2 = (both[0][(i * fields + f) * half_rows : (i * fields + f + 1) * half_rows] for i in (0, 1))
            p3, p4 = (both[1][(i * fields + f) * half_rows : (i * fields + f + 1) * half_rows] for i in (0, 1))
            for upper, even, odd in ((1, p1 - p2, p3 + p4), (0, p1 + p2, p4 - p3)):
                for back, value in ((0, even - odd), (1, even + odd)):
                    for j in range(2):
                        mixed[upper, back, j, f] = jnp.take_along_axis(
                            value, picks[j, f, back], axis=1, mode="promise_in_bounds"
                        )
        inner = lane % 64
        for upper in (0, 1):
            row_tiles = []
            for back in (1, 0):
                pieces = []
                for j in range(2):
                    piece = mixed[upper, back, j, 0]
                    for f in range(1, fields):
                        piece = jnp.where(inner >= f * quarter, mixed[upper, back, j, f], piece)
                    pieces.append(piece)
                row_tiles.append(jnp.concatenate(pieces, axis=1))
            for a in range(lev_count // 2):
                dest = lev_count // 2 + a if upper else lev_count // 2 - 1 - a
                tile = jnp.concatenate([value[4 * a : 4 * a + 4] for value in row_tiles], axis=0)
                send_ref[r, dest] = jnp.where(reach[upper] < lengths[r] - float(points_dev * dest), tile, 0.0)
        started = []
        paired = lev_count & (lev_count - 1) == 0
        for offset in range(lev_count - 1, 0, -1):
            peer = me ^ offset if paired else lax.rem(me + offset, lev_count)
            copy = pltpu.make_async_remote_copy(
                src_ref=send_ref.at[r, peer],
                dst_ref=got_ref.at[r, me],
                send_sem=send_sem.at[r, offset],
                recv_sem=recv_sem.at[r, offset],
                device_id={"lev": peer},
                device_id_type=pl.DeviceIdType.MESH,
            )
            copy.start()
            started.append(copy)
        kept = pltpu.make_async_copy(send_ref.at[r, me], got_ref.at[r, me], own_sem.at[r])
        kept.start()
        started.append(kept)
        copies.append(started)

    upper = me >= lev_count // 2
    span = half_step * group
    width = place_ref.shape[1]
    sub = iota((8, width), 0)
    order = jnp.where(upper, sub, (sub // 4) * 4 + 3 - sub % 4)
    spread_by = jnp.concatenate([place_ref[...], place_ref[...]], axis=0)
    for r in range(cycles):
        for copy in copies[r]:
            copy.wait()
        rows = [[] for _ in range(4)]
        for first in range(0, lev_count, 4):
            for j in range(2):
                at = slice(j * LANES, (j + 1) * LANES)
                low_half, high_half = [], []
                for level in (first, first + 2):
                    one, two = got_ref[r, level, :, at], got_ref[r, level + 1, :, at]
                    turned = pltpu.roll(jnp.where(half_lane, two, one), 64, 1)
                    low_half.append(jnp.where(half_lane, one, turned))
                    high_half.append(jnp.where(half_lane, turned, two))
                rows[2 * j].append(jnp.concatenate(low_half, axis=1))
                rows[2 * j + 1].append(jnp.concatenate(high_half, axis=1))
        high, low = split(jnp.concatenate([row for quads in rows for row in quads], axis=0))
        spread = jnp.dot(jnp.concatenate([high, low], axis=1), spread_by, preferred_element_type=jnp.float32)
        sets = lev_count // 4
        for q in range(4):
            total = spread[8 * sets * q : 8 * sets * q + 8]
            for i in range(1, sets):
                total = total + pltpu.roll(spread[8 * (sets * q + i) : 8 * (sets * q + i) + 8], 4 * fields * i, 1)
            total = jnp.take_along_axis(total, order, axis=0, mode="promise_in_bounds")
            begin = q * quarter * group
            size = min(quarter * group, span - begin)
            for k in range(8):
                s = (k % 2) * 4 + k // 2
                out_ref[r : r + 1, k * span + begin : k * span + begin + size] = total[s : s + 1, :size]


def local(spectral, legendre, slot_wave, cycle_len, lat_order):
    slot_count = spectral.shape[2]
    degrees = spectral.shape[3]
    half_cycles = legendre.shape[1]
    lev_count = lax.axis_size("lev")
    wave_count = lax.axis_size("wave")
    slots = slot_wave.shape[0]
    padded_len = (RMAX + 8 * lev_count - 1) // (8 * lev_count) * 8 * lev_count
    points_dev = padded_len // lev_count
    half_step = points_dev // 8
    parts = spectral.shape[0] * spectral.shape[1]
    fields = parts // 2
    cycles = lat_order.shape[0] // wave_count
    groups = (slot_count + LANES - 1) // LANES
    chunks, left = [], slot_count
    while left:
        size = 64 if 64 < left < slot_count else min(left, 32)
        chunks.append(size)
        left -= size
    half_rows = 2 * lev_count
    counts = (half_step + 15) // 16
    low_at = (16 * counts + LANES - 1) // LANES * LANES

    quarter = (half_step + 3) // 4
    assert fields * quarter <= 64 and half_step <= LANES and lev_count % 4 == 0
    wide = 2 * LANES
    width = (quarter * fields * lev_count + LANES - 1) // LANES * LANES
    vmem = pl.BlockSpec(memory_space=pltpu.VMEM)
    hbm = pl.BlockSpec(memory_space=pl.ANY)
    return pl.pallas_call(
        functools.partial(kernel, half_step, tuple(chunks)),
        out_shape=pltpu.VMEM((cycles, points_dev * lev_count * fields), jnp.float32),
        in_specs=[hbm] * 5,
        out_specs=vmem,
        scratch_shapes=[
            pltpu.VMEM(slot_wave.shape, jnp.int32),
            pltpu.SMEM(lat_order.shape, jnp.int32),
            pltpu.SMEM(cycle_len.shape, jnp.int32),
            pltpu.VMEM((parts, slot_count, degrees), jnp.bfloat16),
            pltpu.VMEM((half_cycles, slot_count, degrees), jnp.bfloat16),
            pltpu.VMEM((groups * LANES, LANES), jnp.float32),
            pltpu.VMEM((2 * half_cycles, 8, LANES), jnp.float32),
            pltpu.VMEM((groups, wave_count, cycles, 8, LANES), jnp.float32),
            pltpu.VMEM((groups, wave_count, cycles, 8, LANES), jnp.float32),
            pltpu.VMEM((cycles, 2, half_rows, slots), jnp.float32),
            pltpu.VMEM((cycles, 8, slots), jnp.float32),
            pltpu.VMEM((cycles, 2, slots // LANES, low_at + 16 * counts, LANES), jnp.bfloat16),
            pltpu.VMEM((2 * LANES, width), jnp.bfloat16),
            pltpu.VMEM((cycles, lev_count, 8, wide), jnp.float32),
            pltpu.VMEM((cycles, lev_count, 8, wide), jnp.float32),
            pltpu.SemaphoreType.DMA((3,)),
            pltpu.SemaphoreType.DMA((2, len(chunks))),
            pltpu.SemaphoreType.DMA((groups,)),
            pltpu.SemaphoreType.DMA((groups, wave_count)),
            pltpu.SemaphoreType.DMA((groups, wave_count)),
            pltpu.SemaphoreType.DMA((cycles,)),
            pltpu.SemaphoreType.DMA((cycles, lev_count)),
            pltpu.SemaphoreType.DMA((cycles, lev_count)),
        ],
        compiler_params=pltpu.CompilerParams(collective_id=0, has_side_effects=True),
        name="transform",
    )(
        slot_wave, lat_order, cycle_len,
        spectral.reshape(parts, slot_count, degrees), jnp.transpose(legendre, (1, 0, 2)),
    )


def solution(mesh):
    in_specs = (P("lev", None, "wave", None), P("wave", None, None), P(), P(), P())
    out_specs = P("wave", "lev")
    return jax.shard_map(local, mesh=mesh, in_specs=in_specs, out_specs=out_specs, check_vma=False)
```

```python
import functools
import math

import jax
import jax.numpy as jnp
from jax import lax
from jax.experimental import pallas as pl
from jax.experimental.pallas import tpu as pltpu
from jax.sharding import PartitionSpec as P

RMAX = 5136
LANES = 128
BLOCK = 16
AHEAD = 3


def split(value):
    high = value.astype(jnp.bfloat16)
    return high, (value - high.astype(jnp.float32)).astype(jnp.bfloat16)


def dot_nt(left, right):
    return lax.dot_general(left, right, (((1,), (1,)), ((), ())), preferred_element_type=jnp.float32)


def turns(t):
    y = math.pi * t
    z = y * y
    sine = jnp.full_like(z, 1.0 / math.factorial(13))
    for n in (11, 9, 7, 5, 3, 1):
        sign = -1.0 if (n // 2) % 2 else 1.0
        sine = sine * z + sign / math.factorial(n)
    sine = sine * y
    cosine = jnp.full_like(z, 1.0 / math.factorial(12))
    for n in (10, 8, 6, 4, 2, 0):
        sign = -1.0 if (n // 2) % 2 else 1.0
        cosine = cosine * z + sign / math.factorial(n)
    return 1.0 - 2.0 * sine * sine, 2.0 * sine * cosine


def iota(shape, dim):
    return lax.broadcasted_iota(jnp.int32, shape, dim)


def kernel(
    half_step, chunks,
    wave_hbm, lat_hbm, cycle_hbm, spec_hbm, leg_hbm, out_ref,
    wave_ref, lat_ref, cycle_ref,
    spec_ref, leg_ref, col_ref, four_ref, wsend_ref, wgot_ref, wsend_last_ref, wgot_last_ref,
    twist_ref, cen_ref, tab_ref, place_ref, send_ref, got_ref,
    small_sem, load_sem, wown_sem, wsend_sem, wrecv_sem, own_sem, send_sem, recv_sem,
):
    parts, slot_count, degrees = spec_ref.shape
    half_cycles = leg_ref.shape[0]
    fields = parts // 2
    wave_count, cycles = wsend_ref.shape[1:3]
    groups = (slot_count + LANES - 1) // LANES
    packed = 0 < slot_count % LANES <= LANES // 2
    lev_count = send_ref.shape[1]
    wide = send_ref.shape[-1]
    slots = wave_ref.shape[0]
    tiles = slots // LANES
    step = 2 * half_step
    points_dev = 4 * step
    half_rows = twist_ref.shape[3]
    blocks = half_rows // 8
    counts = (half_step + 15) // 16
    low_at = tab_ref.shape[3] - 16 * counts
    me = lax.axis_index("lev")
    my_wave = lax.axis_index("wave")
    first_row = my_wave * cycles

    loads, starts = [], []
    start = 0
    for i, size in enumerate(chunks):
        at = pl.ds(start, size)
        loads.append([
            pltpu.make_async_copy(leg_hbm.at[:, at], leg_ref.at[:, at], load_sem.at[0, i]),
            pltpu.make_async_copy(spec_hbm.at[:, at], spec_ref.at[:, at], load_sem.at[1, i]),
        ])
        starts.append(start)
        start += size
    small = [
        pltpu.make_async_copy(source, target, small_sem.at[i])
        for i, (source, target) in enumerate(((wave_hbm, wave_ref), (lat_hbm, lat_ref), (cycle_hbm, cycle_ref)))
    ]
    for copy in small:
        copy.start()
    for pair in loads[:AHEAD]:
        for copy in pair:
            copy.start()
    barrier = pltpu.get_barrier_semaphore()
    for offset in range(1, lev_count):
        peer = lax.rem(me + offset, lev_count)
        pl.semaphore_signal(barrier, inc=1, device_id={"lev": peer}, device_id_type=pl.DeviceIdType.MESH)
    for offset in range(1, wave_count):
        peer = lax.rem(my_wave + offset, wave_count)
        pl.semaphore_signal(barrier, inc=1, device_id={"wave": peer}, device_id_type=pl.DeviceIdType.MESH)
    for copy in small:
        copy.wait()

    waves = wave_ref[...].reshape(1, slots).astype(jnp.float32)

    mine = pltpu.roll(waves, slots - my_wave * slot_count, 1)
    eye = iota((LANES, LANES), 0) == iota((LANES, LANES), 1)
    for g in range(groups):
        column = jnp.sum(jnp.where(eye, mine[:, g * LANES : (g + 1) * LANES], 0.0), axis=1, keepdims=True)
        col_ref[g * LANES : (g + 1) * LANES] = column - iota((LANES, LANES), 1).astype(jnp.float32)

    near = [i + 0.5 for i in range(8)]
    twist = [step * (i + 0.5) for i in range(8)]
    rest = [16.0 * k + 8.0 for k in range(counts)] + [8.0 * step * a for a in range(1, blocks)]
    rest += [(lev_count * points_dev - 1) / 2]
    rest_count = len(rest)
    rest_rows = (rest_count + 7) // 8 * 8
    row = iota((rest_rows, 1), 0)
    row8 = iota((8, 1), 0).astype(jnp.float32) + 0.5
    rest_mult = jnp.zeros((rest_rows, 1), jnp.float32)
    for i, value in enumerate(rest):
        rest_mult = jnp.where(row == i, value, rest_mult)
    mult = jnp.concatenate([row8, row8 * step, rest_mult], axis=0)
    lengths = [
        cycle_ref[lat_ref[first_row + r] % half_cycles].astype(jnp.float32) for r in range(cycles)
    ]
    if low_at > 16 * counts:
        hole = low_at - 16 * counts
        tab_ref[:, :, :, 16 * counts : low_at, :] = jnp.zeros((cycles, 2, tiles, hole, LANES), jnp.bfloat16)

    def tables(r, t):
        at = slice(t * LANES, (t + 1) * LANES)
        wave = waves[:, at]
        length = lengths[r]
        inverse = 1.0 / jnp.full((1, LANES), length)
        phase = wave * mult
        whole = jnp.floor(phase * inverse + 0.5)
        cosine, sine = turns((phase - whole * length) * inverse)
        nc, ns, tc, ts = cosine[0:8], sine[0:8], cosine[8:16], sine[8:16]
        rc, rs = cosine[16:], sine[16:]
        twist_ref[r, 0, t, 0:8, :] = tc
        twist_ref[r, 1, t, 0:8, :] = ts
        for a in range(1, blocks):
            i = counts + a - 1
            c, s = rc[i : i + 1], rs[i : i + 1]
            twist_ref[r, 0, t, 8 * a : 8 * a + 8, :] = tc * c - ts * s
            twist_ref[r, 1, t, 8 * a : 8 * a + 8, :] = ts * c + tc * s
        weight = jnp.where(wave == 0.0, 1.0, 2.0)
        i = rest_count - 1
        cen_ref[r, t, 0:1, :] = rc[i : i + 1] * weight
        cen_ref[r, t, 1:2, :] = rs[i : i + 1] * weight
        for k in range(counts):
            c, s = rc[k : k + 1], rs[k : k + 1]
            cc, ss, sc, cs = c * nc, s * ns, s * nc, c * ns
            for which, value in (
                (0, jnp.concatenate([cc + ss, cc - ss], axis=0)),
                (1, jnp.concatenate([sc - cs, sc + cs], axis=0)),
            ):
                high, low = split(value)
                tab_ref[r, which, t, 16 * k : 16 * k + 16, :] = high
                tab_ref[r, which, t, low_at + 16 * k : low_at + 16 * k + 16, :] = low

    turns_count = LANES // BLOCK
    lane = iota((1, LANES), 1)
    lane_chunk = lane // BLOCK
    flip = jnp.where((iota((BLOCK, LANES), 1) & 1) == 1, -1.0, 1.0).astype(jnp.bfloat16)
    lats = 2 * half_cycles
    own = iota((BLOCK, parts * BLOCK), 0) == iota((BLOCK, parts * BLOCK), 1) % BLOCK
    south_row = iota((lats, 1), 0) >= half_cycles

    def legendre(b):
        at = slice(b * BLOCK, (b + 1) * BLOCK)
        column = col_ref[at, :]
        columns = []
        for d in range(0, degrees, LANES):
            live = jnp.where(column <= float(d), 1.0, 0.0).astype(jnp.bfloat16)
            north = [live * leg_ref[k, at, d : d + LANES] for k in range(half_cycles)]
            columns.append(jnp.concatenate(north + [flip * value for value in north], axis=0))
        rows = jnp.concatenate([spec_ref[(j - b) % parts, at, :] for j in range(parts)], axis=0)
        return dot_nt(jnp.concatenate(columns, axis=1), rows)

    def diagonal(product):
        product = product.reshape(lats, BLOCK, parts * BLOCK)
        total = jnp.sum(jnp.where(own[None], product, 0.0), axis=1)
        return jnp.concatenate([total, jnp.zeros((lats, LANES - parts * BLOCK), jnp.float32)], axis=1)

    wave_paired = wave_count & (wave_count - 1) == 0
    halves = 2 if wave_count == 4 and 2 * slot_count % LANES == 0 else 1
    near = (1,) if halves == 2 else tuple(range(wave_count))
    wave_copies = {False: [], True: []}

    def send_group(g, sums):
        pack = packed and g == groups - 1
        number = mine[:, g * LANES : (g + 1) * LANES]
        if pack:
            number = jnp.where(lane < LANES // 2, number, pltpu.roll(number, LANES // 2, 1))
        sign = jnp.where(south_row & ((number.astype(jnp.int32) & 1) == 1), -1.0, 1.0)
        values = []
        for c in range(parts):
            move = turns_count // 2 if pack and c % 2 else 0
            shifts = {}
            for i, (b, total) in enumerate(sums):
                place = (c + b) % parts
                shifts.setdefault((i + move - place) % turns_count, []).append((i + move, place, total))
            value = None
            for shift, members in shifts.items():
                picked = None
                for i, place, total in members:
                    picked = total if picked is None else jnp.where(lane_chunk == place, total, picked)
                if shift:
                    picked = pltpu.roll(picked, shift * BLOCK, 1)
                if value is None:
                    value = picked
                else:
                    mask = lane_chunk == members[0][0]
                    for i, _, _ in members[1:]:
                        mask = mask | (lane_chunk == i)
                    value = jnp.where(mask, picked, value)
            values.append(value)
        if pack:
            for f in range(fields):
                four_ref[:, f, :] = jnp.where(lane < LANES // 2, values[2 * f], values[2 * f + 1]) * sign
        else:
            for c in range(parts):
                four_ref[:, (c % 2) * 4 + c // 2, :] = values[c] * sign
        for w in range(wave_count):
            for r in range(cycles):
                lat = lat_ref[w * cycles + r]
                if pack:
                    wsend_last_ref[w, r] = four_ref[lat, 0:4, :]
                else:
                    wsend_ref[g, w, r] = four_ref[lat]
        source = wsend_last_ref if pack else wsend_ref.at[g]
        target = wgot_last_ref if pack else wgot_ref.at[g]
        if g == 0:
            pl.semaphore_wait(barrier, lev_count + wave_count - 2)
        for offset in range(wave_count - 1, 0, -1):
            peer = my_wave ^ offset if wave_paired else lax.rem(my_wave + offset, wave_count)
            copy = pltpu.make_async_remote_copy(
                src_ref=source.at[peer],
                dst_ref=target.at[my_wave],
                send_sem=wsend_sem.at[g, offset],
                recv_sem=wrecv_sem.at[g, offset],
                device_id={"wave": peer},
                device_id_type=pl.DeviceIdType.MESH,
            )
            copy.start()
            wave_copies[offset in near].append(copy)
        kept = pltpu.make_async_copy(source.at[my_wave], target.at[my_wave], wown_sem.at[g])
        kept.start()
        wave_copies[1].append(kept)

    early = min(2, cycles)
    for r in range(early):
        for t in range(tiles):
            tables(r, t)
    total_blocks = slot_count // BLOCK
    sums = []

    def finish(b, product):
        sums.append((b, diagonal(product)))
        if b % turns_count == turns_count - 1 or b == total_blocks - 1:
            send_group(b // turns_count, sums)
            sums.clear()

    pending = None
    for b in range(total_blocks):
        if b * BLOCK in starts:
            i = starts.index(b * BLOCK)
            for copy in loads[i]:
                copy.wait()
            for copy in loads[i + AHEAD] if i + AHEAD < len(loads) else ():
                copy.start()
        product = legendre(b)
        if pending is not None:
            finish(*pending)
        pending = (b, product)
    finish(*pending)
    for r in range(early, cycles):
        for t in range(tiles):
            tables(r, t)

    group = lev_count * fields
    quarter = (half_step + 3) // 4
    source = iota((4 * 64, 1), 0)
    inner = source % 64
    target = jnp.where(
        inner < fields * quarter, (inner % quarter) * group + source // 64 * fields + inner // quarter, -1
    )
    for j in range(place_ref.shape[1] // LANES):
        at = slice(j * LANES, (j + 1) * LANES)
        place_ref[:, at] = jnp.where(iota((4 * 64, LANES), 1) + j * LANES == target, 1.0, 0.0).astype(jnp.bfloat16)

    picks = {}
    inner = lane % 64
    for j in range(2):
        for f in range(fields):
            point = inner - f * quarter
            point = (2 * j + lane // 64) * quarter + jnp.clip(point, 0, quarter - 1)
            for back in (0, 1):
                p = half_step - 1 - point if back else point
                p = jnp.clip(p, 0, half_step - 1)
                low = p % 16
                index = p - low + jnp.where(low < 8, 7 - low, low)
                picks[j, f, back] = jnp.broadcast_to(index, (half_rows, LANES))
    where_lane = iota((8, wide), 1)
    where_row = iota((8, wide), 0)
    inner = where_lane % 64
    inside = where_lane // 64 * quarter + inner % quarter
    inside = jnp.where((inner < fields * quarter) & (inside < half_step), inside, 1 << 20)
    reach = {}
    for upper in (0, 1):
        i = where_row % 4 if upper else 3 - where_row % 4
        reach[upper] = (step * i + half_step * (where_row // 4) + inside).astype(jnp.float32)
    half_lane = lane < 64

    copies = []
    turn_sign = jnp.where(iota((8, 1), 0) < 4, -1.0, 1.0)
    half_tiles = tiles // halves
    half_waves = wave_count // halves
    rows = 2 * fields * half_rows

    def transform(r, h):
        side = (my_wave // half_waves) ^ h if halves == 2 else 0
        operands, tabs = ([], []), ([], [])
        for tt in range(half_tiles):
            t = side * half_tiles + tt
            coef = None
            position = tt * LANES
            while position < (tt + 1) * LANES:
                w, inner = side * half_waves + position // slot_count, position % slot_count
                g, start = inner // LANES, inner % LANES
                size = min((tt + 1) * LANES - position, slot_count - inner, LANES - start)
                if packed and g == groups - 1:
                    piece = wgot_last_ref[w, r]
                    piece = jnp.concatenate([piece, pltpu.roll(piece, LANES // 2, 1)], axis=0)
                else:
                    piece = wgot_ref[g, w, r]
                to = position - tt * LANES
                if to != start:
                    piece = pltpu.roll(piece, (to - start) % LANES, 1)
                coef = piece if coef is None else jnp.where(lane >= to, piece, coef)
                position += size
            coef = coef * cen_ref[r, t, 0:1, :] + pltpu.roll(coef, 4, 0) * (cen_ref[r, t, 1:2, :] * turn_sign)
            tc, ts = twist_ref[r, 0, t], twist_ref[r, 1, t]
            pairs = ([], [])
            for first in (0, 1):
                for f in range(fields):
                    part = coef[4 * first + f : 4 * first + f + 1]
                    for which in (0, 1):
                        pairs[which].append(split(part * (tc if which == first else ts)))
            for which in (0, 1):
                operands[which].append(
                    jnp.concatenate([high for high, _ in pairs[which]] + [low for _, low in pairs[which]], axis=0)
                )
                tabs[which].append(tab_ref[r, which, t])
        both = []
        for which in (0, 1):
            product = dot_nt(jnp.concatenate(operands[which], axis=1), jnp.concatenate(tabs[which], axis=1))
            both.append(product[:rows] + product[rows:])
        return both

    for copy in wave_copies[True]:
        copy.wait()
    if halves == 2:
        begun = transform(0, 0)
    for copy in wave_copies[False]:
        copy.wait()

    for r in range(cycles):
        if halves == 2:
            first = begun if r == 0 else transform(r, 0)
            value = [one + two for one, two in zip(first, transform(r, 1))]
        else:
            value = transform(r, 0)
        both = [
            one[:, :LANES]
            + jnp.concatenate([one[:, low_at:], jnp.zeros((rows, low_at - 16 * counts), jnp.float32)], axis=1)
            for one in value
        ]
        mixed = {}
        for f in range(fields):
            p1, p2 = (both[0][(i * fields + f) * half_rows : (i * fields + f + 1) * half_rows] for i in (0, 1))
            p3, p4 = (both[1][(i * fields + f) * half_rows : (i * fields + f + 1) * half_rows] for i in (0, 1))
            for upper, even, odd in ((1, p1 - p2, p3 + p4), (0, p1 + p2, p4 - p3)):
                for back, value in ((0, even - odd), (1, even + odd)):
                    for j in range(2):
                        mixed[upper, back, j, f] = jnp.take_along_axis(
                            value, picks[j, f, back], axis=1, mode="promise_in_bounds"
                        )
        inner = lane % 64
        for upper in (0, 1):
            row_tiles = []
            for back in (1, 0):
                pieces = []
                for j in range(2):
                    piece = mixed[upper, back, j, 0]
                    for f in range(1, fields):
                        piece = jnp.where(inner >= f * quarter, mixed[upper, back, j, f], piece)
                    pieces.append(piece)
                row_tiles.append(jnp.concatenate(pieces, axis=1))
            for a in range(lev_count // 2):
                dest = lev_count // 2 + a if upper else lev_count // 2 - 1 - a
                tile = jnp.concatenate([value[4 * a : 4 * a + 4] for value in row_tiles], axis=0)
                send_ref[r, dest] = jnp.where(reach[upper] < lengths[r] - float(points_dev * dest), tile, 0.0)
        started = []
        paired = lev_count & (lev_count - 1) == 0
        for offset in range(lev_count - 1, 0, -1):
            peer = me ^ offset if paired else lax.rem(me + offset, lev_count)
            copy = pltpu.make_async_remote_copy(
                src_ref=send_ref.at[r, peer],
                dst_ref=got_ref.at[r, me],
                send_sem=send_sem.at[r, offset],
                recv_sem=recv_sem.at[r, offset],
                device_id={"lev": peer},
                device_id_type=pl.DeviceIdType.MESH,
            )
            copy.start()
            started.append(copy)
        kept = pltpu.make_async_copy(send_ref.at[r, me], got_ref.at[r, me], own_sem.at[r])
        kept.start()
        started.append(kept)
        copies.append(started)

    upper = me >= lev_count // 2
    span = half_step * group
    width = place_ref.shape[1]
    sub = iota((8, width), 0)
    order = jnp.where(upper, sub, (sub // 4) * 4 + 3 - sub % 4)
    spread_by = jnp.concatenate([place_ref[...], place_ref[...]], axis=0)
    for r in range(cycles):
        for copy in copies[r]:
            copy.wait()
        rows = [[] for _ in range(4)]
        for first in range(0, lev_count, 4):
            for j in range(2):
                at = slice(j * LANES, (j + 1) * LANES)
                low_half, high_half = [], []
                for level in (first, first + 2):
                    one, two = got_ref[r, level, :, at], got_ref[r, level + 1, :, at]
                    turned = pltpu.roll(jnp.where(half_lane, two, one), 64, 1)
                    low_half.append(jnp.where(half_lane, one, turned))
                    high_half.append(jnp.where(half_lane, turned, two))
                rows[2 * j].append(jnp.concatenate(low_half, axis=1))
                rows[2 * j + 1].append(jnp.concatenate(high_half, axis=1))
        high, low = split(jnp.concatenate([row for quads in rows for row in quads], axis=0))
        spread = jnp.dot(jnp.concatenate([high, low], axis=1), spread_by, preferred_element_type=jnp.float32)
        sets = lev_count // 4
        for q in range(4):
            total = spread[8 * sets * q : 8 * sets * q + 8]
            for i in range(1, sets):
                total = total + pltpu.roll(spread[8 * (sets * q + i) : 8 * (sets * q + i) + 8], 4 * fields * i, 1)
            total = jnp.take_along_axis(total, order, axis=0, mode="promise_in_bounds")
            begin = q * quarter * group
            size = min(quarter * group, span - begin)
            for k in range(8):
                s = (k % 2) * 4 + k // 2
                out_ref[r : r + 1, k * span + begin : k * span + begin + size] = total[s : s + 1, :size]


def local(spectral, legendre, slot_wave, cycle_len, lat_order):
    slot_count = spectral.shape[2]
    degrees = spectral.shape[3]
    half_cycles = legendre.shape[1]
    lev_count = lax.axis_size("lev")
    wave_count = lax.axis_size("wave")
    slots = slot_wave.shape[0]
    padded_len = (RMAX + 8 * lev_count - 1) // (8 * lev_count) * 8 * lev_count
    points_dev = padded_len // lev_count
    half_step = points_dev // 8
    parts = spectral.shape[0] * spectral.shape[1]
    fields = parts // 2
    cycles = lat_order.shape[0] // wave_count
    groups = (slot_count + LANES - 1) // LANES
    chunks, left = [], slot_count
    while left:
        size = 64 if 64 < left < slot_count else min(left, 32)
        chunks.append(size)
        left -= size
    packed = 0 < slot_count % LANES <= LANES // 2
    half_rows = 2 * lev_count
    counts = (half_step + 15) // 16
    low_at = (16 * counts + LANES - 1) // LANES * LANES

    quarter = (half_step + 3) // 4
    assert fields * quarter <= 64 and half_step <= LANES and lev_count % 4 == 0
    wide = 2 * LANES
    width = (quarter * fields * lev_count + LANES - 1) // LANES * LANES
    vmem = pl.BlockSpec(memory_space=pltpu.VMEM)
    hbm = pl.BlockSpec(memory_space=pl.ANY)
    return pl.pallas_call(
        functools.partial(kernel, half_step, tuple(chunks)),
        out_shape=pltpu.VMEM((cycles, points_dev * lev_count * fields), jnp.float32),
        in_specs=[hbm] * 5,
        out_specs=vmem,
        scratch_shapes=[
            pltpu.VMEM(slot_wave.shape, jnp.int32),
            pltpu.SMEM(lat_order.shape, jnp.int32),
            pltpu.SMEM(cycle_len.shape, jnp.int32),
            pltpu.VMEM((parts, slot_count, degrees), jnp.bfloat16),
            pltpu.VMEM((half_cycles, slot_count, degrees), jnp.bfloat16),
            pltpu.VMEM((groups * LANES, LANES), jnp.float32),
            pltpu.VMEM((2 * half_cycles, 8, LANES), jnp.float32),
            pltpu.VMEM((max(1, groups - packed), wave_count, cycles, 8, LANES), jnp.float32),
            pltpu.VMEM((max(1, groups - packed), wave_count, cycles, 8, LANES), jnp.float32),
            pltpu.VMEM((wave_count, cycles, 4, LANES), jnp.float32),
            pltpu.VMEM((wave_count, cycles, 4, LANES), jnp.float32),
            pltpu.VMEM((cycles, 2, slots // LANES, half_rows, LANES), jnp.float32),
            pltpu.VMEM((cycles, slots // LANES, 8, LANES), jnp.float32),
            pltpu.VMEM((cycles, 2, slots // LANES, low_at + 16 * counts, LANES), jnp.bfloat16),
            pltpu.VMEM((2 * LANES, width), jnp.bfloat16),
            pltpu.VMEM((cycles, lev_count, 8, wide), jnp.float32),
            pltpu.VMEM((cycles, lev_count, 8, wide), jnp.float32),
            pltpu.SemaphoreType.DMA((3,)),
            pltpu.SemaphoreType.DMA((2, len(chunks))),
            pltpu.SemaphoreType.DMA((groups,)),
            pltpu.SemaphoreType.DMA((groups, wave_count)),
            pltpu.SemaphoreType.DMA((groups, wave_count)),
            pltpu.SemaphoreType.DMA((cycles,)),
            pltpu.SemaphoreType.DMA((cycles, lev_count)),
            pltpu.SemaphoreType.DMA((cycles, lev_count)),
        ],
        compiler_params=pltpu.CompilerParams(collective_id=0, has_side_effects=True),
        name="transform",
    )(
        slot_wave, lat_order, cycle_len,
        spectral.reshape(parts, slot_count, degrees), jnp.transpose(legendre, (1, 0, 2)),
    )


def solution(mesh):
    in_specs = (P("lev", None, "wave", None), P("wave", None, None), P(), P(), P())
    out_specs = P("wave", "lev")
    return jax.shard_map(local, mesh=mesh, in_specs=in_specs, out_specs=out_specs, check_vma=False)
```

```python
import functools
import math

import jax
import jax.numpy as jnp
from jax import lax
from jax.experimental import pallas as pl
from jax.experimental.pallas import tpu as pltpu
from jax.sharding import PartitionSpec as P

RMAX = 5136
LANES = 128
BLOCK = 16
AHEAD = 2


def split(value):
    high = value.astype(jnp.bfloat16)
    return high, (value - high.astype(jnp.float32)).astype(jnp.bfloat16)


def dot_nt(left, right):
    return lax.dot_general(left, right, (((1,), (1,)), ((), ())), preferred_element_type=jnp.float32)


def turns(t):
    y = math.pi * t
    z = y * y
    sine = jnp.full_like(z, 1.0 / math.factorial(13))
    for n in (11, 9, 7, 5, 3, 1):
        sign = -1.0 if (n // 2) % 2 else 1.0
        sine = sine * z + sign / math.factorial(n)
    sine = sine * y
    cosine = jnp.full_like(z, 1.0 / math.factorial(12))
    for n in (10, 8, 6, 4, 2, 0):
        sign = -1.0 if (n // 2) % 2 else 1.0
        cosine = cosine * z + sign / math.factorial(n)
    return 1.0 - 2.0 * sine * sine, 2.0 * sine * cosine


def iota(shape, dim):
    return lax.broadcasted_iota(jnp.int32, shape, dim)


def kernel(
    half_step, chunks,
    wave_hbm, lat_hbm, cycle_hbm, spec_hbm, leg_hbm, out_ref,
    wave_ref, lat_ref, cycle_ref,
    spec_ref, leg_ref, col_ref, four_ref, wsend_ref, wgot_ref, wsend_last_ref, wgot_last_ref,
    twist_ref, cen_ref, tab_ref, place_ref, send_ref, got_ref,
    small_sem, load_sem, wown_sem, wsend_sem, wrecv_sem, own_sem, send_sem, recv_sem,
):
    parts, slot_count, degrees = spec_ref.shape
    half_cycles = leg_ref.shape[0]
    fields = parts // 2
    wave_count, cycles = wsend_ref.shape[1:3]
    groups = (slot_count + LANES - 1) // LANES
    packed = 0 < slot_count % LANES <= LANES // 2
    lev_count = send_ref.shape[1]
    wide = send_ref.shape[-1]
    slots = wave_ref.shape[0]
    tiles = slots // LANES
    step = 2 * half_step
    points_dev = 4 * step
    half_rows = twist_ref.shape[3]
    blocks = half_rows // 8
    counts = (half_step + 15) // 16
    low_at = tab_ref.shape[3] - 16 * counts
    me = lax.axis_index("lev")
    my_wave = lax.axis_index("wave")
    first_row = my_wave * cycles

    loads, starts = [], []
    start = 0
    for i, size in enumerate(chunks):
        at = pl.ds(start, size)
        loads.append([
            pltpu.make_async_copy(leg_hbm.at[:, at], leg_ref.at[:, at], load_sem.at[0, i]),
            pltpu.make_async_copy(spec_hbm.at[:, at], spec_ref.at[:, at], load_sem.at[1, i]),
        ])
        starts.append(start)
        start += size
    small = [
        pltpu.make_async_copy(source, target, small_sem.at[i])
        for i, (source, target) in enumerate(((wave_hbm, wave_ref), (lat_hbm, lat_ref), (cycle_hbm, cycle_ref)))
    ]
    for copy in small:
        copy.start()
    for pair in loads[:AHEAD]:
        for copy in pair:
            copy.start()
    barrier = pltpu.get_barrier_semaphore()
    for offset in range(1, lev_count):
        peer = lax.rem(me + offset, lev_count)
        pl.semaphore_signal(barrier, inc=1, device_id={"lev": peer}, device_id_type=pl.DeviceIdType.MESH)
    for offset in range(1, wave_count):
        peer = lax.rem(my_wave + offset, wave_count)
        pl.semaphore_signal(barrier, inc=1, device_id={"wave": peer}, device_id_type=pl.DeviceIdType.MESH)
    for copy in small:
        copy.wait()

    waves = wave_ref[...].reshape(1, slots).astype(jnp.float32)

    mine = pltpu.roll(waves, slots - my_wave * slot_count, 1)
    eye = iota((LANES, LANES), 0) == iota((LANES, LANES), 1)
    for g in range(groups):
        column = jnp.sum(jnp.where(eye, mine[:, g * LANES : (g + 1) * LANES], 0.0), axis=1, keepdims=True)
        col_ref[g * LANES : (g + 1) * LANES] = column - iota((LANES, LANES), 1).astype(jnp.float32)

    near = [i + 0.5 for i in range(8)]
    twist = [step * (i + 0.5) for i in range(8)]
    rest = [16.0 * k + 8.0 for k in range(counts)] + [8.0 * step * a for a in range(1, blocks)]
    rest += [(lev_count * points_dev - 1) / 2]
    rest_count = len(rest)
    rest_rows = (rest_count + 7) // 8 * 8
    row = iota((rest_rows, 1), 0)
    row8 = iota((8, 1), 0).astype(jnp.float32) + 0.5
    rest_mult = jnp.zeros((rest_rows, 1), jnp.float32)
    for i, value in enumerate(rest):
        rest_mult = jnp.where(row == i, value, rest_mult)
    mult = jnp.concatenate([row8, row8 * step, rest_mult], axis=0)
    lengths = [
        cycle_ref[lat_ref[first_row + r] % half_cycles].astype(jnp.float32) for r in range(cycles)
    ]
    if low_at > 16 * counts:
        hole = low_at - 16 * counts
        tab_ref[:, :, :, 16 * counts : low_at, :] = jnp.zeros((cycles, 2, tiles, hole, LANES), jnp.bfloat16)

    def tables(r, t):
        at = slice(t * LANES, (t + 1) * LANES)
        wave = waves[:, at]
        length = lengths[r]
        inverse = 1.0 / jnp.full((1, LANES), length)
        phase = wave * mult
        whole = jnp.floor(phase * inverse + 0.5)
        cosine, sine = turns((phase - whole * length) * inverse)
        nc, ns, tc, ts = cosine[0:8], sine[0:8], cosine[8:16], sine[8:16]
        rc, rs = cosine[16:], sine[16:]
        twist_ref[r, 0, t, 0:8, :] = tc
        twist_ref[r, 1, t, 0:8, :] = ts
        for a in range(1, blocks):
            i = counts + a - 1
            c, s = rc[i : i + 1], rs[i : i + 1]
            twist_ref[r, 0, t, 8 * a : 8 * a + 8, :] = tc * c - ts * s
            twist_ref[r, 1, t, 8 * a : 8 * a + 8, :] = ts * c + tc * s
        weight = jnp.where(wave == 0.0, 1.0, 2.0)
        i = rest_count - 1
        cen_ref[r, t, 0:1, :] = rc[i : i + 1] * weight
        cen_ref[r, t, 1:2, :] = rs[i : i + 1] * weight
        for k in range(counts):
            c, s = rc[k : k + 1], rs[k : k + 1]
            cc, ss, sc, cs = c * nc, s * ns, s * nc, c * ns
            for which, value in (
                (0, jnp.concatenate([cc + ss, cc - ss], axis=0)),
                (1, jnp.concatenate([sc - cs, sc + cs], axis=0)),
            ):
                high, low = split(value)
                tab_ref[r, which, t, 16 * k : 16 * k + 16, :] = high
                tab_ref[r, which, t, low_at + 16 * k : low_at + 16 * k + 16, :] = low

    turns_count = LANES // BLOCK
    lane = iota((1, LANES), 1)
    lane_chunk = lane // BLOCK
    flip = jnp.where((iota((BLOCK, LANES), 1) & 1) == 1, -1.0, 1.0).astype(jnp.bfloat16)
    lats = 2 * half_cycles
    own = iota((BLOCK, parts * BLOCK), 0) == iota((BLOCK, parts * BLOCK), 1) % BLOCK
    south_row = iota((lats, 1), 0) >= half_cycles

    def legendre(b):
        at = slice(b * BLOCK, (b + 1) * BLOCK)
        column = col_ref[at, :]
        columns = []
        for d in range(0, degrees, LANES):
            live = jnp.where(column <= float(d), 1.0, 0.0).astype(jnp.bfloat16)
            north = [live * leg_ref[k, at, d : d + LANES] for k in range(half_cycles)]
            columns.append(jnp.concatenate(north + [flip * value for value in north], axis=0))
        rows = jnp.concatenate([spec_ref[(j - b) % parts, at, :] for j in range(parts)], axis=0)
        return dot_nt(jnp.concatenate(columns, axis=1), rows)

    def diagonal(product):
        product = product.reshape(lats, BLOCK, parts * BLOCK)
        total = jnp.sum(jnp.where(own[None], product, 0.0), axis=1)
        return jnp.concatenate([total, jnp.zeros((lats, LANES - parts * BLOCK), jnp.float32)], axis=1)

    wave_paired = wave_count & (wave_count - 1) == 0
    halves = 2 if wave_count == 4 and 2 * slot_count % LANES == 0 else 1
    near = (1,) if halves == 2 else tuple(range(wave_count))
    wave_copies = {False: [], True: []}

    def send_group(g, sums):
        pack = packed and g == groups - 1
        number = mine[:, g * LANES : (g + 1) * LANES]
        if pack:
            number = jnp.where(lane < LANES // 2, number, pltpu.roll(number, LANES // 2, 1))
        sign = jnp.where(south_row & ((number.astype(jnp.int32) & 1) == 1), -1.0, 1.0)
        values = []
        for c in range(parts):
            move = turns_count // 2 if pack and c % 2 else 0
            shifts = {}
            for i, (b, total) in enumerate(sums):
                place = (c + b) % parts
                shifts.setdefault((i + move - place) % turns_count, []).append((i + move, place, total))
            value = None
            for shift, members in shifts.items():
                picked = None
                for i, place, total in members:
                    picked = total if picked is None else jnp.where(lane_chunk == place, total, picked)
                if shift:
                    picked = pltpu.roll(picked, shift * BLOCK, 1)
                if value is None:
                    value = picked
                else:
                    mask = lane_chunk == members[0][0]
                    for i, _, _ in members[1:]:
                        mask = mask | (lane_chunk == i)
                    value = jnp.where(mask, picked, value)
            values.append(value)
        if pack:
            for f in range(fields):
                four_ref[:, f, :] = jnp.where(lane < LANES // 2, values[2 * f], values[2 * f + 1]) * sign
        else:
            for c in range(parts):
                four_ref[:, (c % 2) * 4 + c // 2, :] = values[c] * sign
        for w in range(wave_count):
            for r in range(cycles):
                lat = lat_ref[w * cycles + r]
                if pack:
                    wsend_last_ref[w, r] = four_ref[lat, 0:4, :]
                else:
                    wsend_ref[g, w, r] = four_ref[lat]
        source = wsend_last_ref if pack else wsend_ref.at[g]
        target = wgot_last_ref if pack else wgot_ref.at[g]
        if g == 0:
            pl.semaphore_wait(barrier, lev_count + wave_count - 2)
        for offset in range(wave_count - 1, 0, -1):
            peer = my_wave ^ offset if wave_paired else lax.rem(my_wave + offset, wave_count)
            copy = pltpu.make_async_remote_copy(
                src_ref=source.at[peer],
                dst_ref=target.at[my_wave],
                send_sem=wsend_sem.at[g, offset],
                recv_sem=wrecv_sem.at[g, offset],
                device_id={"wave": peer},
                device_id_type=pl.DeviceIdType.MESH,
            )
            copy.start()
            wave_copies[offset in near].append(copy)
        kept = pltpu.make_async_copy(source.at[my_wave], target.at[my_wave], wown_sem.at[g])
        kept.start()
        wave_copies[1].append(kept)

    early = min(1, cycles)
    for r in range(early):
        for t in range(tiles):
            tables(r, t)
    total_blocks = slot_count // BLOCK
    sums = []

    def finish(b, product):
        sums.append((b, diagonal(product)))
        if b % turns_count == turns_count - 1 or b == total_blocks - 1:
            send_group(b // turns_count, sums)
            sums.clear()

    pending = None
    for b in range(total_blocks):
        if b * BLOCK in starts:
            i = starts.index(b * BLOCK)
            for copy in loads[i]:
                copy.wait()
            for copy in loads[i + AHEAD] if i + AHEAD < len(loads) else ():
                copy.start()
        product = legendre(b)
        if pending is not None:
            finish(*pending)
        pending = (b, product)
    finish(*pending)
    for r in range(early, cycles):
        for t in range(tiles):
            tables(r, t)

    group = lev_count * fields
    quarter = (half_step + 3) // 4
    source = iota((4 * 64, 1), 0)
    inner = source % 64
    target = jnp.where(
        inner < fields * quarter, (inner % quarter) * group + source // 64 * fields + inner // quarter, -1
    )
    for j in range(place_ref.shape[1] // LANES):
        at = slice(j * LANES, (j + 1) * LANES)
        place_ref[:, at] = jnp.where(iota((4 * 64, LANES), 1) + j * LANES == target, 1.0, 0.0).astype(jnp.bfloat16)

    picks = {}
    inner = lane % 64
    for j in range(2):
        for f in range(fields):
            point = inner - f * quarter
            point = (2 * j + lane // 64) * quarter + jnp.clip(point, 0, quarter - 1)
            for back in (0, 1):
                p = half_step - 1 - point if back else point
                p = jnp.clip(p, 0, half_step - 1)
                low = p % 16
                index = p - low + jnp.where(low < 8, 7 - low, low)
                picks[j, f, back] = jnp.broadcast_to(index, (half_rows, LANES))
    where_lane = iota((8, wide), 1)
    where_row = iota((8, wide), 0)
    inner = where_lane % 64
    inside = where_lane // 64 * quarter + inner % quarter
    inside = jnp.where((inner < fields * quarter) & (inside < half_step), inside, 1 << 20)
    reach = {}
    for upper in (0, 1):
        i = where_row % 4 if upper else 3 - where_row % 4
        reach[upper] = (step * i + half_step * (where_row // 4) + inside).astype(jnp.float32)
    half_lane = lane < 64

    copies = []
    turn_sign = jnp.where(iota((8, 1), 0) < 4, -1.0, 1.0)
    half_tiles = tiles // halves
    half_waves = wave_count // halves
    rows = 2 * fields * half_rows

    def transform(r, h):
        side = (my_wave // half_waves) ^ h if halves == 2 else 0
        operands, tabs = ([], []), ([], [])
        for tt in range(half_tiles):
            t = side * half_tiles + tt
            coef = None
            position = tt * LANES
            while position < (tt + 1) * LANES:
                w, inner = side * half_waves + position // slot_count, position % slot_count
                g, start = inner // LANES, inner % LANES
                size = min((tt + 1) * LANES - position, slot_count - inner, LANES - start)
                if packed and g == groups - 1:
                    piece = wgot_last_ref[w, r]
                    piece = jnp.concatenate([piece, pltpu.roll(piece, LANES // 2, 1)], axis=0)
                else:
                    piece = wgot_ref[g, w, r]
                to = position - tt * LANES
                if to != start:
                    piece = pltpu.roll(piece, (to - start) % LANES, 1)
                coef = piece if coef is None else jnp.where(lane >= to, piece, coef)
                position += size
            coef = coef * cen_ref[r, t, 0:1, :] + pltpu.roll(coef, 4, 0) * (cen_ref[r, t, 1:2, :] * turn_sign)
            tc, ts = twist_ref[r, 0, t], twist_ref[r, 1, t]
            pairs = ([], [])
            for first in (0, 1):
                for f in range(fields):
                    part = coef[4 * first + f : 4 * first + f + 1]
                    for which in (0, 1):
                        pairs[which].append(split(part * (tc if which == first else ts)))
            for which in (0, 1):
                operands[which].append(
                    jnp.concatenate([high for high, _ in pairs[which]] + [low for _, low in pairs[which]], axis=0)
                )
                tabs[which].append(tab_ref[r, which, t])
        both = []
        for which in (0, 1):
            product = dot_nt(jnp.concatenate(operands[which], axis=1), jnp.concatenate(tabs[which], axis=1))
            both.append(product[:rows] + product[rows:])
        return both

    for copy in wave_copies[True]:
        copy.wait()
    if halves == 2:
        begun = transform(0, 0)
    for copy in wave_copies[False]:
        copy.wait()

    for r in range(cycles):
        if halves == 2:
            first = begun if r == 0 else transform(r, 0)
            value = [one + two for one, two in zip(first, transform(r, 1))]
        else:
            value = transform(r, 0)
        both = [
            one[:, :LANES]
            + jnp.concatenate([one[:, low_at:], jnp.zeros((rows, low_at - 16 * counts), jnp.float32)], axis=1)
            for one in value
        ]
        mixed = {}
        for f in range(fields):
            p1, p2 = (both[0][(i * fields + f) * half_rows : (i * fields + f + 1) * half_rows] for i in (0, 1))
            p3, p4 = (both[1][(i * fields + f) * half_rows : (i * fields + f + 1) * half_rows] for i in (0, 1))
            for upper, even, odd in ((1, p1 - p2, p3 + p4), (0, p1 + p2, p4 - p3)):
                for back, value in ((0, even - odd), (1, even + odd)):
                    for j in range(2):
                        mixed[upper, back, j, f] = jnp.take_along_axis(
                            value, picks[j, f, back], axis=1, mode="promise_in_bounds"
                        )
        inner = lane % 64
        for upper in (0, 1):
            row_tiles = []
            for back in (1, 0):
                pieces = []
                for j in range(2):
                    piece = mixed[upper, back, j, 0]
                    for f in range(1, fields):
                        piece = jnp.where(inner >= f * quarter, mixed[upper, back, j, f], piece)
                    pieces.append(piece)
                row_tiles.append(jnp.concatenate(pieces, axis=1))
            for a in range(lev_count // 2):
                dest = lev_count // 2 + a if upper else lev_count // 2 - 1 - a
                tile = jnp.concatenate([value[4 * a : 4 * a + 4] for value in row_tiles], axis=0)
                send_ref[r, dest] = jnp.where(reach[upper] < lengths[r] - float(points_dev * dest), tile, 0.0)
        started = []
        paired = lev_count & (lev_count - 1) == 0
        for offset in range(lev_count - 1, 0, -1):
            peer = me ^ offset if paired else lax.rem(me + offset, lev_count)
            copy = pltpu.make_async_remote_copy(
                src_ref=send_ref.at[r, peer],
                dst_ref=got_ref.at[r, me],
                send_sem=send_sem.at[r, offset],
                recv_sem=recv_sem.at[r, offset],
                device_id={"lev": peer},
                device_id_type=pl.DeviceIdType.MESH,
            )
            copy.start()
            started.append(copy)
        kept = pltpu.make_async_copy(send_ref.at[r, me], got_ref.at[r, me], own_sem.at[r])
        kept.start()
        started.append(kept)
        copies.append(started)

    upper = me >= lev_count // 2
    span = half_step * group
    width = place_ref.shape[1]
    sub = iota((8, width), 0)
    order = jnp.where(upper, sub, (sub // 4) * 4 + 3 - sub % 4)
    spread_by = jnp.concatenate([place_ref[...], place_ref[...]], axis=0)
    for r in range(cycles):
        for copy in copies[r]:
            copy.wait()
        rows = [[] for _ in range(4)]
        for first in range(0, lev_count, 4):
            for j in range(2):
                at = slice(j * LANES, (j + 1) * LANES)
                low_half, high_half = [], []
                for level in (first, first + 2):
                    one, two = got_ref[r, level, :, at], got_ref[r, level + 1, :, at]
                    turned = pltpu.roll(jnp.where(half_lane, two, one), 64, 1)
                    low_half.append(jnp.where(half_lane, one, turned))
                    high_half.append(jnp.where(half_lane, turned, two))
                rows[2 * j].append(jnp.concatenate(low_half, axis=1))
                rows[2 * j + 1].append(jnp.concatenate(high_half, axis=1))
        high, low = split(jnp.concatenate([row for quads in rows for row in quads], axis=0))
        spread = jnp.dot(jnp.concatenate([high, low], axis=1), spread_by, preferred_element_type=jnp.float32)
        sets = lev_count // 4
        for q in range(4):
            total = spread[8 * sets * q : 8 * sets * q + 8]
            for i in range(1, sets):
                total = total + pltpu.roll(spread[8 * (sets * q + i) : 8 * (sets * q + i) + 8], 4 * fields * i, 1)
            total = jnp.take_along_axis(total, order, axis=0, mode="promise_in_bounds")
            begin = q * quarter * group
            size = min(quarter * group, span - begin)
            for k in range(8):
                s = (k % 2) * 4 + k // 2
                out_ref[r : r + 1, k * span + begin : k * span + begin + size] = total[s : s + 1, :size]


def local(spectral, legendre, slot_wave, cycle_len, lat_order):
    slot_count = spectral.shape[2]
    degrees = spectral.shape[3]
    half_cycles = legendre.shape[1]
    lev_count = lax.axis_size("lev")
    wave_count = lax.axis_size("wave")
    slots = slot_wave.shape[0]
    padded_len = (RMAX + 8 * lev_count - 1) // (8 * lev_count) * 8 * lev_count
    points_dev = padded_len // lev_count
    half_step = points_dev // 8
    parts = spectral.shape[0] * spectral.shape[1]
    fields = parts // 2
    cycles = lat_order.shape[0] // wave_count
    groups = (slot_count + LANES - 1) // LANES
    edge = max(BLOCK, slot_count // 5 // BLOCK * BLOCK)
    middle = max(0, slot_count - 2 * edge)
    chunks = [edge, middle // 2 // BLOCK * BLOCK]
    chunks += [middle - chunks[1], slot_count - edge - middle]
    chunks = [size for size in chunks if size > 0]
    packed = 0 < slot_count % LANES <= LANES // 2
    half_rows = 2 * lev_count
    counts = (half_step + 15) // 16
    low_at = (16 * counts + LANES - 1) // LANES * LANES

    quarter = (half_step + 3) // 4
    assert fields * quarter <= 64 and half_step <= LANES and lev_count % 4 == 0
    wide = 2 * LANES
    width = (quarter * fields * lev_count + LANES - 1) // LANES * LANES
    vmem = pl.BlockSpec(memory_space=pltpu.VMEM)
    hbm = pl.BlockSpec(memory_space=pl.ANY)
    return pl.pallas_call(
        functools.partial(kernel, half_step, tuple(chunks)),
        out_shape=pltpu.VMEM((cycles, points_dev * lev_count * fields), jnp.float32),
        in_specs=[hbm] * 5,
        out_specs=vmem,
        scratch_shapes=[
            pltpu.VMEM(slot_wave.shape, jnp.int32),
            pltpu.SMEM(lat_order.shape, jnp.int32),
            pltpu.SMEM(cycle_len.shape, jnp.int32),
            pltpu.VMEM((parts, slot_count, degrees), jnp.bfloat16),
            pltpu.VMEM((half_cycles, slot_count, degrees), jnp.bfloat16),
            pltpu.VMEM((groups * LANES, LANES), jnp.float32),
            pltpu.VMEM((2 * half_cycles, 8, LANES), jnp.float32),
            pltpu.VMEM((max(1, groups - packed), wave_count, cycles, 8, LANES), jnp.float32),
            pltpu.VMEM((max(1, groups - packed), wave_count, cycles, 8, LANES), jnp.float32),
            pltpu.VMEM((wave_count, cycles, 4, LANES), jnp.float32),
            pltpu.VMEM((wave_count, cycles, 4, LANES), jnp.float32),
            pltpu.VMEM((cycles, 2, slots // LANES, half_rows, LANES), jnp.float32),
            pltpu.VMEM((cycles, slots // LANES, 8, LANES), jnp.float32),
            pltpu.VMEM((cycles, 2, slots // LANES, low_at + 16 * counts, LANES), jnp.bfloat16),
            pltpu.VMEM((2 * LANES, width), jnp.bfloat16),
            pltpu.VMEM((cycles, lev_count, 8, wide), jnp.float32),
            pltpu.VMEM((cycles, lev_count, 8, wide), jnp.float32),
            pltpu.SemaphoreType.DMA((3,)),
            pltpu.SemaphoreType.DMA((2, len(chunks))),
            pltpu.SemaphoreType.DMA((groups,)),
            pltpu.SemaphoreType.DMA((groups, wave_count)),
            pltpu.SemaphoreType.DMA((groups, wave_count)),
            pltpu.SemaphoreType.DMA((cycles,)),
            pltpu.SemaphoreType.DMA((cycles, lev_count)),
            pltpu.SemaphoreType.DMA((cycles, lev_count)),
        ],
        compiler_params=pltpu.CompilerParams(collective_id=0, has_side_effects=True),
        name="transform",
    )(
        slot_wave, lat_order, cycle_len,
        spectral.reshape(parts, slot_count, degrees), jnp.transpose(legendre, (1, 0, 2)),
    )


def solution(mesh):
    in_specs = (P("lev", None, "wave", None), P("wave", None, None), P(), P(), P())
    out_specs = P("wave", "lev")
    return jax.shard_map(local, mesh=mesh, in_specs=in_specs, out_specs=out_specs, check_vma=False)
```

```python
import functools
import math

import jax
import jax.numpy as jnp
from jax import lax
from jax.experimental import pallas as pl
from jax.experimental.pallas import tpu as pltpu
from jax.sharding import PartitionSpec as P

RMAX = 5136
LANES = 128
BLOCK = 16
AHEAD = 2


def split(value):
    high = value.astype(jnp.bfloat16)
    return high, (value - high.astype(jnp.float32)).astype(jnp.bfloat16)


def dot_nt(left, right):
    return lax.dot_general(left, right, (((1,), (1,)), ((), ())), preferred_element_type=jnp.float32)


def turns(t):
    y = math.pi * t
    z = y * y
    sine = jnp.full_like(z, 1.0 / math.factorial(13))
    for n in (11, 9, 7, 5, 3, 1):
        sign = -1.0 if (n // 2) % 2 else 1.0
        sine = sine * z + sign / math.factorial(n)
    sine = sine * y
    cosine = jnp.full_like(z, 1.0 / math.factorial(12))
    for n in (10, 8, 6, 4, 2, 0):
        sign = -1.0 if (n // 2) % 2 else 1.0
        cosine = cosine * z + sign / math.factorial(n)
    return 1.0 - 2.0 * sine * sine, 2.0 * sine * cosine


def iota(shape, dim):
    return lax.broadcasted_iota(jnp.int32, shape, dim)


def kernel(
    half_step, chunks,
    wave_hbm, lat_hbm, cycle_hbm, spec_hbm, leg_hbm, out_ref,
    wave_ref, lat_ref, cycle_ref,
    spec_ref, leg_ref, col_ref, four_ref, wsend_ref, wgot_ref, wsend_last_ref, wgot_last_ref,
    twist_ref, cen_ref, tab_ref, place_ref, send_ref, got_ref,
    small_sem, load_sem, wown_sem, wsend_sem, wrecv_sem, own_sem, send_sem, recv_sem,
):
    parts, slot_count, degrees = spec_ref.shape
    half_cycles = leg_ref.shape[0]
    fields = parts // 2
    wave_count, cycles = wsend_ref.shape[1:3]
    groups = (slot_count + LANES - 1) // LANES
    packed = 0 < slot_count % LANES <= LANES // 2
    lev_count = send_ref.shape[1]
    wide = send_ref.shape[-1]
    slots = wave_ref.shape[0]
    tiles = slots // LANES
    step = 2 * half_step
    points_dev = 4 * step
    half_rows = twist_ref.shape[3]
    blocks = half_rows // 8
    counts = (half_step + 15) // 16
    low_at = tab_ref.shape[3] - 16 * counts
    me = lax.axis_index("lev")
    my_wave = lax.axis_index("wave")
    first_row = my_wave * cycles

    loads, starts = [], []
    start = 0
    for i, size in enumerate(chunks):
        at = pl.ds(start, size)
        loads.append([
            pltpu.make_async_copy(leg_hbm.at[:, at], leg_ref.at[:, at], load_sem.at[0, i]),
            pltpu.make_async_copy(spec_hbm.at[:, at], spec_ref.at[:, at], load_sem.at[1, i]),
        ])
        starts.append(start)
        start += size
    small = [
        pltpu.make_async_copy(source, target, small_sem.at[i])
        for i, (source, target) in enumerate(((wave_hbm, wave_ref), (lat_hbm, lat_ref), (cycle_hbm, cycle_ref)))
    ]
    for copy in small:
        copy.start()
    for pair in loads[:AHEAD]:
        for copy in pair:
            copy.start()
    barrier = pltpu.get_barrier_semaphore()
    for offset in range(1, lev_count):
        peer = lax.rem(me + offset, lev_count)
        pl.semaphore_signal(barrier, inc=1, device_id={"lev": peer}, device_id_type=pl.DeviceIdType.MESH)
    for offset in range(1, wave_count):
        peer = lax.rem(my_wave + offset, wave_count)
        pl.semaphore_signal(barrier, inc=1, device_id={"wave": peer}, device_id_type=pl.DeviceIdType.MESH)
    for copy in small:
        copy.wait()

    waves = wave_ref[...].reshape(1, slots).astype(jnp.float32)

    mine = pltpu.roll(waves, slots - my_wave * slot_count, 1)
    eye = iota((LANES, LANES), 0) == iota((LANES, LANES), 1)
    for g in range(groups):
        column = jnp.sum(jnp.where(eye, mine[:, g * LANES : (g + 1) * LANES], 0.0), axis=1, keepdims=True)
        col_ref[g * LANES : (g + 1) * LANES] = column - iota((LANES, LANES), 1).astype(jnp.float32)

    near = [i + 0.5 for i in range(8)]
    twist = [step * (i + 0.5) for i in range(8)]
    rest = [16.0 * k + 8.0 for k in range(counts)] + [8.0 * step * a for a in range(1, blocks)]
    rest += [(lev_count * points_dev - 1) / 2]
    rest_count = len(rest)
    rest_rows = (rest_count + 7) // 8 * 8
    row = iota((rest_rows, 1), 0)
    row8 = iota((8, 1), 0).astype(jnp.float32) + 0.5
    rest_mult = jnp.zeros((rest_rows, 1), jnp.float32)
    for i, value in enumerate(rest):
        rest_mult = jnp.where(row == i, value, rest_mult)
    mult = jnp.concatenate([row8, row8 * step, rest_mult], axis=0)
    lengths = [
        cycle_ref[lat_ref[first_row + r] % half_cycles].astype(jnp.float32) for r in range(cycles)
    ]
    if low_at > 16 * counts:
        hole = low_at - 16 * counts
        tab_ref[:, :, :, 16 * counts : low_at, :] = jnp.zeros((cycles, 2, tiles, hole, LANES), jnp.bfloat16)

    def tables(r, t):
        at = slice(t * LANES, (t + 1) * LANES)
        wave = waves[:, at]
        length = lengths[r]
        inverse = 1.0 / jnp.full((1, LANES), length)
        phase = wave * mult
        whole = jnp.floor(phase * inverse + 0.5)
        cosine, sine = turns((phase - whole * length) * inverse)
        nc, ns, tc, ts = cosine[0:8], sine[0:8], cosine[8:16], sine[8:16]
        rc, rs = cosine[16:], sine[16:]
        twist_ref[r, 0, t, 0:8, :] = tc
        twist_ref[r, 1, t, 0:8, :] = ts
        for a in range(1, blocks):
            i = counts + a - 1
            c, s = rc[i : i + 1], rs[i : i + 1]
            twist_ref[r, 0, t, 8 * a : 8 * a + 8, :] = tc * c - ts * s
            twist_ref[r, 1, t, 8 * a : 8 * a + 8, :] = ts * c + tc * s
        weight = jnp.where(wave == 0.0, 1.0, 2.0)
        i = rest_count - 1
        cen_ref[r, t, 0:1, :] = rc[i : i + 1] * weight
        cen_ref[r, t, 1:2, :] = rs[i : i + 1] * weight
        for k in range(counts):
            c, s = rc[k : k + 1], rs[k : k + 1]
            cc, ss, sc, cs = c * nc, s * ns, s * nc, c * ns
            for which, value in (
                (0, jnp.concatenate([cc + ss, cc - ss], axis=0)),
                (1, jnp.concatenate([sc - cs, sc + cs], axis=0)),
            ):
                high, low = split(value)
                tab_ref[r, which, t, 16 * k : 16 * k + 16, :] = high
                tab_ref[r, which, t, low_at + 16 * k : low_at + 16 * k + 16, :] = low

    turns_count = LANES // BLOCK
    lane = iota((1, LANES), 1)
    lane_chunk = lane // BLOCK
    flip = jnp.where((iota((BLOCK, LANES), 1) & 1) == 1, -1.0, 1.0).astype(jnp.bfloat16)
    lats = 2 * half_cycles
    own = iota((BLOCK, parts * BLOCK), 0) == iota((BLOCK, parts * BLOCK), 1) % BLOCK
    south_row = iota((lats, 1), 0) >= half_cycles

    def legendre(b):
        at = slice(b * BLOCK, (b + 1) * BLOCK)
        column = col_ref[at, :]
        columns = []
        for d in range(0, degrees, LANES):
            live = jnp.where(column <= float(d), 1.0, 0.0).astype(jnp.bfloat16)
            north = [live * leg_ref[k, at, d : d + LANES] for k in range(half_cycles)]
            columns.append(jnp.concatenate(north + [flip * value for value in north], axis=0))
        rows = jnp.concatenate([spec_ref[(j - b) % parts, at, :] for j in range(parts)], axis=0)
        return dot_nt(jnp.concatenate(columns, axis=1), rows)

    def diagonal(product):
        product = product.reshape(lats, BLOCK, parts * BLOCK)
        total = jnp.sum(jnp.where(own[None], product, 0.0), axis=1)
        return jnp.concatenate([total, jnp.zeros((lats, LANES - parts * BLOCK), jnp.float32)], axis=1)

    wave_paired = wave_count & (wave_count - 1) == 0
    halves = 2 if wave_count == 4 and 2 * slot_count % LANES == 0 else 1
    near = (1,) if halves == 2 else tuple(range(wave_count))
    wave_copies = {False: [], True: []}

    def send_group(g, sums):
        pack = packed and g == groups - 1
        number = mine[:, g * LANES : (g + 1) * LANES]
        if pack:
            number = jnp.where(lane < LANES // 2, number, pltpu.roll(number, LANES // 2, 1))
        sign = jnp.where(south_row & ((number.astype(jnp.int32) & 1) == 1), -1.0, 1.0)
        values = []
        for c in range(parts):
            move = turns_count // 2 if pack and c % 2 else 0
            shifts = {}
            for i, (b, total) in enumerate(sums):
                place = (c + b) % parts
                shifts.setdefault((i + move - place) % turns_count, []).append((i + move, place, total))
            value = None
            for shift, members in shifts.items():
                picked = None
                for i, place, total in members:
                    picked = total if picked is None else jnp.where(lane_chunk == place, total, picked)
                if shift:
                    picked = pltpu.roll(picked, shift * BLOCK, 1)
                if value is None:
                    value = picked
                else:
                    mask = lane_chunk == members[0][0]
                    for i, _, _ in members[1:]:
                        mask = mask | (lane_chunk == i)
                    value = jnp.where(mask, picked, value)
            values.append(value)
        if pack:
            for f in range(fields):
                four_ref[:, f, :] = jnp.where(lane < LANES // 2, values[2 * f], values[2 * f + 1]) * sign
        else:
            for c in range(parts):
                four_ref[:, (c % 2) * 4 + c // 2, :] = values[c] * sign
        for w in range(wave_count):
            for r in range(cycles):
                lat = lat_ref[w * cycles + r]
                if pack:
                    wsend_last_ref[w, r] = four_ref[lat, 0:4, :]
                else:
                    wsend_ref[g, w, r] = four_ref[lat]
        source = wsend_last_ref if pack else wsend_ref.at[g]
        target = wgot_last_ref if pack else wgot_ref.at[g]
        if g == 0:
            pl.semaphore_wait(barrier, lev_count + wave_count - 2)
        for offset in range(wave_count - 1, 0, -1):
            peer = my_wave ^ offset if wave_paired else lax.rem(my_wave + offset, wave_count)
            copy = pltpu.make_async_remote_copy(
                src_ref=source.at[peer],
                dst_ref=target.at[my_wave],
                send_sem=wsend_sem.at[g, offset],
                recv_sem=wrecv_sem.at[g, offset],
                device_id={"wave": peer},
                device_id_type=pl.DeviceIdType.MESH,
            )
            copy.start()
            wave_copies[offset in near].append(copy)
        kept = pltpu.make_async_copy(source.at[my_wave], target.at[my_wave], wown_sem.at[g])
        kept.start()
        wave_copies[1].append(kept)

    early = min(1, cycles)
    for r in range(early):
        for t in range(tiles):
            tables(r, t)
    total_blocks = slot_count // BLOCK
    sums = []

    def finish(b, product):
        sums.append((b, diagonal(product)))
        if b % turns_count == turns_count - 1 or b == total_blocks - 1:
            send_group(b // turns_count, sums)
            sums.clear()

    pending = None
    for b in range(total_blocks):
        if b * BLOCK in starts:
            if pending is not None and b % turns_count == 0:
                finish(*pending)
                pending = None
            i = starts.index(b * BLOCK)
            for copy in loads[i]:
                copy.wait()
            for copy in loads[i + AHEAD] if i + AHEAD < len(loads) else ():
                copy.start()
        product = legendre(b)
        if pending is not None:
            finish(*pending)
        pending = (b, product)
    finish(*pending)
    for r in range(early, cycles):
        for t in range(tiles):
            tables(r, t)

    group = lev_count * fields
    quarter = (half_step + 3) // 4
    source = iota((4 * 64, 1), 0)
    inner = source % 64
    target = jnp.where(
        inner < fields * quarter, (inner % quarter) * group + source // 64 * fields + inner // quarter, -1
    )
    for j in range(place_ref.shape[1] // LANES):
        at = slice(j * LANES, (j + 1) * LANES)
        place_ref[:, at] = jnp.where(iota((4 * 64, LANES), 1) + j * LANES == target, 1.0, 0.0).astype(jnp.bfloat16)

    picks = {}
    inner = lane % 64
    for j in range(2):
        for f in range(fields):
            point = inner - f * quarter
            point = (2 * j + lane // 64) * quarter + jnp.clip(point, 0, quarter - 1)
            for back in (0, 1):
                p = half_step - 1 - point if back else point
                p = jnp.clip(p, 0, half_step - 1)
                low = p % 16
                index = p - low + jnp.where(low < 8, 7 - low, low)
                picks[j, f, back] = jnp.broadcast_to(index, (half_rows, LANES))
    where_lane = iota((8, wide), 1)
    where_row = iota((8, wide), 0)
    inner = where_lane % 64
    inside = where_lane // 64 * quarter + inner % quarter
    inside = jnp.where((inner < fields * quarter) & (inside < half_step), inside, 1 << 20)
    reach = {}
    for upper in (0, 1):
        i = where_row % 4 if upper else 3 - where_row % 4
        reach[upper] = (step * i + half_step * (where_row // 4) + inside).astype(jnp.float32)
    half_lane = lane < 64

    copies = []
    turn_sign = jnp.where(iota((8, 1), 0) < 4, -1.0, 1.0)
    half_tiles = tiles // halves
    half_waves = wave_count // halves
    rows = 2 * fields * half_rows

    def transform(r, h):
        side = (my_wave // half_waves) ^ h if halves == 2 else 0
        operands, tabs = ([], []), ([], [])
        for tt in range(half_tiles):
            t = side * half_tiles + tt
            coef = None
            position = tt * LANES
            while position < (tt + 1) * LANES:
                w, inner = side * half_waves + position // slot_count, position % slot_count
                g, start = inner // LANES, inner % LANES
                size = min((tt + 1) * LANES - position, slot_count - inner, LANES - start)
                if packed and g == groups - 1:
                    piece = wgot_last_ref[w, r]
                    piece = jnp.concatenate([piece, pltpu.roll(piece, LANES // 2, 1)], axis=0)
                else:
                    piece = wgot_ref[g, w, r]
                to = position - tt * LANES
                if to != start:
                    piece = pltpu.roll(piece, (to - start) % LANES, 1)
                coef = piece if coef is None else jnp.where(lane >= to, piece, coef)
                position += size
            coef = coef * cen_ref[r, t, 0:1, :] + pltpu.roll(coef, 4, 0) * (cen_ref[r, t, 1:2, :] * turn_sign)
            tc, ts = twist_ref[r, 0, t], twist_ref[r, 1, t]
            pairs = ([], [])
            for first in (0, 1):
                for f in range(fields):
                    part = coef[4 * first + f : 4 * first + f + 1]
                    for which in (0, 1):
                        pairs[which].append(split(part * (tc if which == first else ts)))
            for which in (0, 1):
                operands[which].append(
                    jnp.concatenate([high for high, _ in pairs[which]] + [low for _, low in pairs[which]], axis=0)
                )
                tabs[which].append(tab_ref[r, which, t])
        both = []
        for which in (0, 1):
            product = dot_nt(jnp.concatenate(operands[which], axis=1), jnp.concatenate(tabs[which], axis=1))
            both.append(product[:rows] + product[rows:])
        return both

    for copy in wave_copies[True]:
        copy.wait()
    if halves == 2:
        begun = transform(0, 0)
    for copy in wave_copies[False]:
        copy.wait()

    for r in range(cycles):
        if halves == 2:
            first = begun if r == 0 else transform(r, 0)
            value = [one + two for one, two in zip(first, transform(r, 1))]
        else:
            value = transform(r, 0)
        both = [
            one[:, :LANES]
            + jnp.concatenate([one[:, low_at:], jnp.zeros((rows, low_at - 16 * counts), jnp.float32)], axis=1)
            for one in value
        ]
        mixed = {}
        for f in range(fields):
            p1, p2 = (both[0][(i * fields + f) * half_rows : (i * fields + f + 1) * half_rows] for i in (0, 1))
            p3, p4 = (both[1][(i * fields + f) * half_rows : (i * fields + f + 1) * half_rows] for i in (0, 1))
            for upper, even, odd in ((1, p1 - p2, p3 + p4), (0, p1 + p2, p4 - p3)):
                for back, value in ((0, even - odd), (1, even + odd)):
                    for j in range(2):
                        mixed[upper, back, j, f] = jnp.take_along_axis(
                            value, picks[j, f, back], axis=1, mode="promise_in_bounds"
                        )
        inner = lane % 64
        for upper in (0, 1):
            row_tiles = []
            for back in (1, 0):
                pieces = []
                for j in range(2):
                    piece = mixed[upper, back, j, 0]
                    for f in range(1, fields):
                        piece = jnp.where(inner >= f * quarter, mixed[upper, back, j, f], piece)
                    pieces.append(piece)
                row_tiles.append(jnp.concatenate(pieces, axis=1))
            for a in range(lev_count // 2):
                dest = lev_count // 2 + a if upper else lev_count // 2 - 1 - a
                tile = jnp.concatenate([value[4 * a : 4 * a + 4] for value in row_tiles], axis=0)
                send_ref[r, dest] = jnp.where(reach[upper] < lengths[r] - float(points_dev * dest), tile, 0.0)
        started = []
        paired = lev_count & (lev_count - 1) == 0
        for offset in range(lev_count - 1, 0, -1):
            peer = me ^ offset if paired else lax.rem(me + offset, lev_count)
            copy = pltpu.make_async_remote_copy(
                src_ref=send_ref.at[r, peer],
                dst_ref=got_ref.at[r, me],
                send_sem=send_sem.at[r, offset],
                recv_sem=recv_sem.at[r, offset],
                device_id={"lev": peer},
                device_id_type=pl.DeviceIdType.MESH,
            )
            copy.start()
            started.append(copy)
        kept = pltpu.make_async_copy(send_ref.at[r, me], got_ref.at[r, me], own_sem.at[r])
        kept.start()
        started.append(kept)
        copies.append(started)

    upper = me >= lev_count // 2
    span = half_step * group
    width = place_ref.shape[1]
    sub = iota((8, width), 0)
    order = jnp.where(upper, sub, (sub // 4) * 4 + 3 - sub % 4)
    spread_by = jnp.concatenate([place_ref[...], place_ref[...]], axis=0)
    for r in range(cycles):
        for copy in copies[r]:
            copy.wait()
        rows = [[] for _ in range(4)]
        for first in range(0, lev_count, 4):
            for j in range(2):
                at = slice(j * LANES, (j + 1) * LANES)
                low_half, high_half = [], []
                for level in (first, first + 2):
                    one, two = got_ref[r, level, :, at], got_ref[r, level + 1, :, at]
                    turned = pltpu.roll(jnp.where(half_lane, two, one), 64, 1)
                    low_half.append(jnp.where(half_lane, one, turned))
                    high_half.append(jnp.where(half_lane, turned, two))
                rows[2 * j].append(jnp.concatenate(low_half, axis=1))
                rows[2 * j + 1].append(jnp.concatenate(high_half, axis=1))
        high, low = split(jnp.concatenate([row for quads in rows for row in quads], axis=0))
        spread = jnp.dot(jnp.concatenate([high, low], axis=1), spread_by, preferred_element_type=jnp.float32)
        sets = lev_count // 4
        for q in range(4):
            total = spread[8 * sets * q : 8 * sets * q + 8]
            for i in range(1, sets):
                total = total + pltpu.roll(spread[8 * (sets * q + i) : 8 * (sets * q + i) + 8], 4 * fields * i, 1)
            total = jnp.take_along_axis(total, order, axis=0, mode="promise_in_bounds")
            begin = q * quarter * group
            size = min(quarter * group, span - begin)
            for k in range(8):
                s = (k % 2) * 4 + k // 2
                out_ref[r : r + 1, k * span + begin : k * span + begin + size] = total[s : s + 1, :size]


def local(spectral, legendre, slot_wave, cycle_len, lat_order):
    slot_count = spectral.shape[2]
    degrees = spectral.shape[3]
    half_cycles = legendre.shape[1]
    lev_count = lax.axis_size("lev")
    wave_count = lax.axis_size("wave")
    slots = slot_wave.shape[0]
    padded_len = (RMAX + 8 * lev_count - 1) // (8 * lev_count) * 8 * lev_count
    points_dev = padded_len // lev_count
    half_step = points_dev // 8
    parts = spectral.shape[0] * spectral.shape[1]
    fields = parts // 2
    cycles = lat_order.shape[0] // wave_count
    groups = (slot_count + LANES - 1) // LANES
    edge = max(BLOCK, slot_count // 5 // BLOCK * BLOCK)
    middle = max(0, slot_count - 2 * edge)
    chunks = [edge, middle // 2 // BLOCK * BLOCK]
    chunks += [middle - chunks[1], slot_count - edge - middle]
    chunks = [size for size in chunks if size > 0]
    packed = 0 < slot_count % LANES <= LANES // 2
    half_rows = 2 * lev_count
    counts = (half_step + 15) // 16
    low_at = (16 * counts + LANES - 1) // LANES * LANES

    quarter = (half_step + 3) // 4
    assert fields * quarter <= 64 and half_step <= LANES and lev_count % 4 == 0
    wide = 2 * LANES
    width = (quarter * fields * lev_count + LANES - 1) // LANES * LANES
    vmem = pl.BlockSpec(memory_space=pltpu.VMEM)
    hbm = pl.BlockSpec(memory_space=pl.ANY)
    return pl.pallas_call(
        functools.partial(kernel, half_step, tuple(chunks)),
        out_shape=pltpu.VMEM((cycles, points_dev * lev_count * fields), jnp.float32),
        in_specs=[hbm] * 5,
        out_specs=vmem,
        scratch_shapes=[
            pltpu.VMEM(slot_wave.shape, jnp.int32),
            pltpu.SMEM(lat_order.shape, jnp.int32),
            pltpu.SMEM(cycle_len.shape, jnp.int32),
            pltpu.VMEM((parts, slot_count, degrees), jnp.bfloat16),
            pltpu.VMEM((half_cycles, slot_count, degrees), jnp.bfloat16),
            pltpu.VMEM((groups * LANES, LANES), jnp.float32),
            pltpu.VMEM((2 * half_cycles, 8, LANES), jnp.float32),
            pltpu.VMEM((max(1, groups - packed), wave_count, cycles, 8, LANES), jnp.float32),
            pltpu.VMEM((max(1, groups - packed), wave_count, cycles, 8, LANES), jnp.float32),
            pltpu.VMEM((wave_count, cycles, 4, LANES), jnp.float32),
            pltpu.VMEM((wave_count, cycles, 4, LANES), jnp.float32),
            pltpu.VMEM((cycles, 2, slots // LANES, half_rows, LANES), jnp.float32),
            pltpu.VMEM((cycles, slots // LANES, 8, LANES), jnp.float32),
            pltpu.VMEM((cycles, 2, slots // LANES, low_at + 16 * counts, LANES), jnp.bfloat16),
            pltpu.VMEM((2 * LANES, width), jnp.bfloat16),
            pltpu.VMEM((cycles, lev_count, 8, wide), jnp.float32),
            pltpu.VMEM((cycles, lev_count, 8, wide), jnp.float32),
            pltpu.SemaphoreType.DMA((3,)),
            pltpu.SemaphoreType.DMA((2, len(chunks))),
            pltpu.SemaphoreType.DMA((groups,)),
            pltpu.SemaphoreType.DMA((groups, wave_count)),
            pltpu.SemaphoreType.DMA((groups, wave_count)),
            pltpu.SemaphoreType.DMA((cycles,)),
            pltpu.SemaphoreType.DMA((cycles, lev_count)),
            pltpu.SemaphoreType.DMA((cycles, lev_count)),
        ],
        compiler_params=pltpu.CompilerParams(collective_id=0, has_side_effects=True),
        name="transform",
    )(
        slot_wave, lat_order, cycle_len,
        spectral.reshape(parts, slot_count, degrees), jnp.transpose(legendre, (1, 0, 2)),
    )


def solution(mesh):
    in_specs = (P("lev", None, "wave", None), P("wave", None, None), P(), P(), P())
    out_specs = P("wave", "lev")
    return jax.shard_map(local, mesh=mesh, in_specs=in_specs, out_specs=out_specs, check_vma=False)
```

```python
import functools
import math

import jax
import jax.numpy as jnp
from jax import lax
from jax.experimental import pallas as pl
from jax.experimental.pallas import tpu as pltpu
from jax.sharding import PartitionSpec as P

RMAX = 5136
LANES = 128
BLOCK = 16
AHEAD = 2


def split(value):
    high = value.astype(jnp.bfloat16)
    return high, (value - high.astype(jnp.float32)).astype(jnp.bfloat16)


def dot_nt(left, right):
    return lax.dot_general(left, right, (((1,), (1,)), ((), ())), preferred_element_type=jnp.float32)


def turns(t):
    y = math.pi * t
    z = y * y
    sine = jnp.full_like(z, 1.0 / math.factorial(13))
    for n in (11, 9, 7, 5, 3, 1):
        sign = -1.0 if (n // 2) % 2 else 1.0
        sine = sine * z + sign / math.factorial(n)
    sine = sine * y
    cosine = jnp.full_like(z, 1.0 / math.factorial(12))
    for n in (10, 8, 6, 4, 2, 0):
        sign = -1.0 if (n // 2) % 2 else 1.0
        cosine = cosine * z + sign / math.factorial(n)
    return 1.0 - 2.0 * sine * sine, 2.0 * sine * cosine


def iota(shape, dim):
    return lax.broadcasted_iota(jnp.int32, shape, dim)


def kernel(
    half_step, chunks,
    wave_hbm, lat_hbm, cycle_hbm, spec_hbm, leg_hbm, out_ref,
    wave_ref, lat_ref, cycle_ref,
    spec_ref, leg_ref, col_ref, four_ref, wsend_ref, wgot_ref, wsend_last_ref, wgot_last_ref,
    twist_ref, cen_ref, tab_ref, place_ref, send_ref, got_ref,
    small_sem, load_sem, wown_sem, wsend_sem, wrecv_sem, own_sem, send_sem, recv_sem,
):
    parts, slot_count, degrees = spec_ref.shape
    half_cycles = leg_ref.shape[0]
    fields = parts // 2
    wave_count, cycles = wsend_ref.shape[1:3]
    groups = (slot_count + LANES - 1) // LANES
    packed = 0 < slot_count % LANES <= LANES // 2
    lev_count = send_ref.shape[1]
    wide = send_ref.shape[-1]
    slots = wave_ref.shape[0]
    tiles = slots // LANES
    step = 2 * half_step
    points_dev = 4 * step
    half_rows = twist_ref.shape[3]
    blocks = half_rows // 8
    counts = (half_step + 15) // 16
    low_at = tab_ref.shape[3] - 16 * counts
    me = lax.axis_index("lev")
    my_wave = lax.axis_index("wave")
    first_row = my_wave * cycles

    loads, starts = [], []
    start = 0
    for i, size in enumerate(chunks):
        at = pl.ds(start, size)
        loads.append([
            pltpu.make_async_copy(leg_hbm.at[:, at], leg_ref.at[:, at], load_sem.at[0, i]),
            pltpu.make_async_copy(spec_hbm.at[:, at], spec_ref.at[:, at], load_sem.at[1, i]),
        ])
        starts.append(start)
        start += size
    small = [
        pltpu.make_async_copy(source, target, small_sem.at[i])
        for i, (source, target) in enumerate(((wave_hbm, wave_ref), (lat_hbm, lat_ref), (cycle_hbm, cycle_ref)))
    ]
    for copy in small:
        copy.start()
    for pair in loads[:AHEAD]:
        for copy in pair:
            copy.start()
    barrier = pltpu.get_barrier_semaphore()
    for offset in range(1, lev_count):
        peer = lax.rem(me + offset, lev_count)
        pl.semaphore_signal(barrier, inc=1, device_id={"lev": peer}, device_id_type=pl.DeviceIdType.MESH)
    for offset in range(1, wave_count):
        peer = lax.rem(my_wave + offset, wave_count)
        pl.semaphore_signal(barrier, inc=1, device_id={"wave": peer}, device_id_type=pl.DeviceIdType.MESH)
    for copy in small:
        copy.wait()

    waves = wave_ref[...].reshape(1, slots).astype(jnp.float32)

    mine = pltpu.roll(waves, slots - my_wave * slot_count, 1)
    eye = iota((LANES, LANES), 0) == iota((LANES, LANES), 1)
    for g in range(groups):
        column = jnp.sum(jnp.where(eye, mine[:, g * LANES : (g + 1) * LANES], 0.0), axis=1, keepdims=True)
        col_ref[g * LANES : (g + 1) * LANES] = column - iota((LANES, LANES), 1).astype(jnp.float32)

    near = [i + 0.5 for i in range(8)]
    twist = [step * (i + 0.5) for i in range(8)]
    rest = [16.0 * k + 8.0 for k in range(counts)] + [8.0 * step * a for a in range(1, blocks)]
    rest += [(lev_count * points_dev - 1) / 2]
    rest_count = len(rest)
    rest_rows = (rest_count + 7) // 8 * 8
    row = iota((rest_rows, 1), 0)
    row8 = iota((8, 1), 0).astype(jnp.float32) + 0.5
    rest_mult = jnp.zeros((rest_rows, 1), jnp.float32)
    for i, value in enumerate(rest):
        rest_mult = jnp.where(row == i, value, rest_mult)
    mult = jnp.concatenate([row8, row8 * step, rest_mult], axis=0)
    lengths = [
        cycle_ref[lat_ref[first_row + r] % half_cycles].astype(jnp.float32) for r in range(cycles)
    ]
    if low_at > 16 * counts:
        hole = low_at - 16 * counts
        tab_ref[:, :, :, 16 * counts : low_at, :] = jnp.zeros((cycles, 2, tiles, hole, LANES), jnp.bfloat16)

    def tables(r, t):
        at = slice(t * LANES, (t + 1) * LANES)
        wave = waves[:, at]
        length = lengths[r]
        inverse = 1.0 / jnp.full((1, LANES), length)
        phase = wave * mult
        whole = jnp.floor(phase * inverse + 0.5)
        cosine, sine = turns((phase - whole * length) * inverse)
        nc, ns, tc, ts = cosine[0:8], sine[0:8], cosine[8:16], sine[8:16]
        rc, rs = cosine[16:], sine[16:]
        twist_ref[r, 0, t, 0:8, :] = tc
        twist_ref[r, 1, t, 0:8, :] = ts
        for a in range(1, blocks):
            i = counts + a - 1
            c, s = rc[i : i + 1], rs[i : i + 1]
            twist_ref[r, 0, t, 8 * a : 8 * a + 8, :] = tc * c - ts * s
            twist_ref[r, 1, t, 8 * a : 8 * a + 8, :] = ts * c + tc * s
        weight = jnp.where(wave == 0.0, 1.0, 2.0)
        i = rest_count - 1
        cen_ref[r, t, 0:1, :] = rc[i : i + 1] * weight
        cen_ref[r, t, 1:2, :] = rs[i : i + 1] * weight
        for k in range(counts):
            c, s = rc[k : k + 1], rs[k : k + 1]
            cc, ss, sc, cs = c * nc, s * ns, s * nc, c * ns
            for which, value in (
                (0, jnp.concatenate([cc + ss, cc - ss], axis=0)),
                (1, jnp.concatenate([sc - cs, sc + cs], axis=0)),
            ):
                high, low = split(value)
                tab_ref[r, which, t, 16 * k : 16 * k + 16, :] = high
                tab_ref[r, which, t, low_at + 16 * k : low_at + 16 * k + 16, :] = low

    turns_count = LANES // BLOCK
    lane = iota((1, LANES), 1)
    lane_chunk = lane // BLOCK
    flip = jnp.where((iota((BLOCK, LANES), 1) & 1) == 1, -1.0, 1.0).astype(jnp.bfloat16)
    lats = 2 * half_cycles
    own = iota((BLOCK, parts * BLOCK), 0) == iota((BLOCK, parts * BLOCK), 1) % BLOCK
    south_row = iota((lats, 1), 0) >= half_cycles

    def legendre(b):
        at = slice(b * BLOCK, (b + 1) * BLOCK)
        column = col_ref[at, :]
        columns = []
        for d in range(0, degrees, LANES):
            live = jnp.where(column <= float(d), 1.0, 0.0).astype(jnp.bfloat16)
            north = [live * leg_ref[k, at, d : d + LANES] for k in range(half_cycles)]
            columns.append(jnp.concatenate(north + [flip * value for value in north], axis=0))
        rows = jnp.concatenate([spec_ref[(j - b) % parts, at, :] for j in range(parts)], axis=0)
        return dot_nt(jnp.concatenate(columns, axis=1), rows)

    def diagonal(product):
        product = product.reshape(lats, BLOCK, parts * BLOCK)
        total = jnp.sum(jnp.where(own[None], product, 0.0), axis=1)
        return jnp.concatenate([total, jnp.zeros((lats, LANES - parts * BLOCK), jnp.float32)], axis=1)

    wave_paired = wave_count & (wave_count - 1) == 0
    halves = 2 if wave_count == 4 and 2 * slot_count % LANES == 0 else 1
    near = (1,) if halves == 2 else tuple(range(wave_count))
    wave_copies = {False: [], True: []}

    def send_group(g, sums):
        pack = packed and g == groups - 1
        number = mine[:, g * LANES : (g + 1) * LANES]
        if pack:
            number = jnp.where(lane < LANES // 2, number, pltpu.roll(number, LANES // 2, 1))
        sign = jnp.where(south_row & ((number.astype(jnp.int32) & 1) == 1), -1.0, 1.0)
        values = []
        for c in range(parts):
            move = turns_count // 2 if pack and c % 2 else 0
            shifts = {}
            for i, (b, total) in enumerate(sums):
                place = (c + b) % parts
                shifts.setdefault((i + move - place) % turns_count, []).append((i + move, place, total))
            value = None
            for shift, members in shifts.items():
                picked = None
                for i, place, total in members:
                    picked = total if picked is None else jnp.where(lane_chunk == place, total, picked)
                if shift:
                    picked = pltpu.roll(picked, shift * BLOCK, 1)
                if value is None:
                    value = picked
                else:
                    mask = lane_chunk == members[0][0]
                    for i, _, _ in members[1:]:
                        mask = mask | (lane_chunk == i)
                    value = jnp.where(mask, picked, value)
            values.append(value)
        if pack:
            for f in range(fields):
                four_ref[:, f, :] = jnp.where(lane < LANES // 2, values[2 * f], values[2 * f + 1]) * sign
        else:
            for c in range(parts):
                four_ref[:, (c % 2) * 4 + c // 2, :] = values[c] * sign
        for w in range(wave_count):
            for r in range(cycles):
                lat = lat_ref[w * cycles + r]
                if pack:
                    wsend_last_ref[w, r] = four_ref[lat, 0:4, :]
                else:
                    wsend_ref[g, w, r] = four_ref[lat]
        source = wsend_last_ref if pack else wsend_ref.at[g]
        target = wgot_last_ref if pack else wgot_ref.at[g]
        if g == 0:
            pl.semaphore_wait(barrier, lev_count + wave_count - 2)
        for offset in range(wave_count - 1, 0, -1):
            peer = my_wave ^ offset if wave_paired else lax.rem(my_wave + offset, wave_count)
            copy = pltpu.make_async_remote_copy(
                src_ref=source.at[peer],
                dst_ref=target.at[my_wave],
                send_sem=wsend_sem.at[g, offset],
                recv_sem=wrecv_sem.at[g, offset],
                device_id={"wave": peer},
                device_id_type=pl.DeviceIdType.MESH,
            )
            copy.start()
            wave_copies[offset in near].append(copy)
        kept = pltpu.make_async_copy(source.at[my_wave], target.at[my_wave], wown_sem.at[g])
        kept.start()
        wave_copies[1].append(kept)

    early = min(1, cycles)
    for r in range(early):
        for t in range(tiles):
            tables(r, t)
    total_blocks = slot_count // BLOCK
    sums = []

    def finish(b, product):
        sums.append((b, diagonal(product)))
        if b % turns_count == turns_count - 1 or b == total_blocks - 1:
            send_group(b // turns_count, sums)
            sums.clear()

    pending = None
    for b in range(total_blocks):
        if b * BLOCK in starts:
            if pending is not None and b % turns_count == 0:
                finish(*pending)
                pending = None
            i = starts.index(b * BLOCK)
            for copy in loads[i]:
                copy.wait()
            for copy in loads[i + AHEAD] if i + AHEAD < len(loads) else ():
                copy.start()
        product = legendre(b)
        if pending is not None:
            finish(*pending)
        pending = (b, product)
    finish(*pending)
    for r in range(early, cycles):
        for t in range(tiles):
            tables(r, t)

    group = lev_count * fields
    quarter = (half_step + 3) // 4
    source = iota((4 * 64, 1), 0)
    inner = source % 64
    target = jnp.where(
        inner < fields * quarter, (inner % quarter) * group + source // 64 * fields + inner // quarter, -1
    )
    for j in range(place_ref.shape[1] // LANES):
        at = slice(j * LANES, (j + 1) * LANES)
        place_ref[:, at] = jnp.where(iota((4 * 64, LANES), 1) + j * LANES == target, 1.0, 0.0).astype(jnp.bfloat16)

    picks = {}
    inner = lane % 64
    for j in range(2):
        for f in range(fields):
            point = inner - f * quarter
            point = (2 * j + lane // 64) * quarter + jnp.clip(point, 0, quarter - 1)
            for back in (0, 1):
                p = half_step - 1 - point if back else point
                p = jnp.clip(p, 0, half_step - 1)
                low = p % 16
                index = p - low + jnp.where(low < 8, 7 - low, low)
                picks[j, f, back] = jnp.broadcast_to(index, (half_rows, LANES))
    where_lane = iota((8, wide), 1)
    where_row = iota((8, wide), 0)
    inner = where_lane % 64
    inside = where_lane // 64 * quarter + inner % quarter
    inside = jnp.where((inner < fields * quarter) & (inside < half_step), inside, 1 << 20)
    reach = {}
    for upper in (0, 1):
        i = where_row % 4 if upper else 3 - where_row % 4
        reach[upper] = (step * i + half_step * (where_row // 4) + inside).astype(jnp.float32)
    half_lane = lane < 64

    copies = []
    turn_sign = jnp.where(iota((8, 1), 0) < 4, -1.0, 1.0)
    half_tiles = tiles // halves
    half_waves = wave_count // halves
    rows = 2 * fields * half_rows

    def transform(r, h):
        side = (my_wave // half_waves) ^ h if halves == 2 else 0
        operands, tabs = ([], []), ([], [])
        for tt in range(half_tiles):
            t = side * half_tiles + tt
            coef = None
            position = tt * LANES
            while position < (tt + 1) * LANES:
                w, inner = side * half_waves + position // slot_count, position % slot_count
                g, start = inner // LANES, inner % LANES
                size = min((tt + 1) * LANES - position, slot_count - inner, LANES - start)
                if packed and g == groups - 1:
                    piece = wgot_last_ref[w, r]
                    piece = jnp.concatenate([piece, pltpu.roll(piece, LANES // 2, 1)], axis=0)
                else:
                    piece = wgot_ref[g, w, r]
                to = position - tt * LANES
                if to != start:
                    piece = pltpu.roll(piece, (to - start) % LANES, 1)
                coef = piece if coef is None else jnp.where(lane >= to, piece, coef)
                position += size
            coef = coef * cen_ref[r, t, 0:1, :] + pltpu.roll(coef, 4, 0) * (cen_ref[r, t, 1:2, :] * turn_sign)
            tc, ts = twist_ref[r, 0, t], twist_ref[r, 1, t]
            pairs = ([], [])
            for first in (0, 1):
                for f in range(fields):
                    part = coef[4 * first + f : 4 * first + f + 1]
                    for which in (0, 1):
                        pairs[which].append(split(part * (tc if which == first else ts)))
            for which in (0, 1):
                operands[which].append(
                    jnp.concatenate([high for high, _ in pairs[which]] + [low for _, low in pairs[which]], axis=0)
                )
                tabs[which].append(tab_ref[r, which, t])
        both = []
        for which in (0, 1):
            product = dot_nt(jnp.concatenate(operands[which], axis=1), jnp.concatenate(tabs[which], axis=1))
            both.append(product[:rows] + product[rows:])
        return both

    for copy in wave_copies[True]:
        copy.wait()
    if halves == 2:
        begun = [transform(r, 0) for r in range(cycles)]
    for copy in wave_copies[False]:
        copy.wait()

    for r in range(cycles):
        if halves == 2:
            first = begun[r]
            value = [one + two for one, two in zip(first, transform(r, 1))]
        else:
            value = transform(r, 0)
        both = [
            one[:, :LANES]
            + jnp.concatenate([one[:, low_at:], jnp.zeros((rows, low_at - 16 * counts), jnp.float32)], axis=1)
            for one in value
        ]
        mixed = {}
        for f in range(fields):
            p1, p2 = (both[0][(i * fields + f) * half_rows : (i * fields + f + 1) * half_rows] for i in (0, 1))
            p3, p4 = (both[1][(i * fields + f) * half_rows : (i * fields + f + 1) * half_rows] for i in (0, 1))
            for upper, even, odd in ((1, p1 - p2, p3 + p4), (0, p1 + p2, p4 - p3)):
                for back, value in ((0, even - odd), (1, even + odd)):
                    for j in range(2):
                        mixed[upper, back, j, f] = jnp.take_along_axis(
                            value, picks[j, f, back], axis=1, mode="promise_in_bounds"
                        )
        inner = lane % 64
        for upper in (0, 1):
            row_tiles = []
            for back in (1, 0):
                pieces = []
                for j in range(2):
                    piece = mixed[upper, back, j, 0]
                    for f in range(1, fields):
                        piece = jnp.where(inner >= f * quarter, mixed[upper, back, j, f], piece)
                    pieces.append(piece)
                row_tiles.append(jnp.concatenate(pieces, axis=1))
            for a in range(lev_count // 2):
                dest = lev_count // 2 + a if upper else lev_count // 2 - 1 - a
                tile = jnp.concatenate([value[4 * a : 4 * a + 4] for value in row_tiles], axis=0)
                send_ref[r, dest] = jnp.where(reach[upper] < lengths[r] - float(points_dev * dest), tile, 0.0)
        started = []
        paired = lev_count & (lev_count - 1) == 0
        for offset in range(lev_count - 1, 0, -1):
            peer = me ^ offset if paired else lax.rem(me + offset, lev_count)
            copy = pltpu.make_async_remote_copy(
                src_ref=send_ref.at[r, peer],
                dst_ref=got_ref.at[r, me],
                send_sem=send_sem.at[r, offset],
                recv_sem=recv_sem.at[r, offset],
                device_id={"lev": peer},
                device_id_type=pl.DeviceIdType.MESH,
            )
            copy.start()
            started.append(copy)
        kept = pltpu.make_async_copy(send_ref.at[r, me], got_ref.at[r, me], own_sem.at[r])
        kept.start()
        started.append(kept)
        copies.append(started)

    upper = me >= lev_count // 2
    span = half_step * group
    width = place_ref.shape[1]
    sub = iota((8, width), 0)
    order = jnp.where(upper, sub, (sub // 4) * 4 + 3 - sub % 4)
    spread_by = jnp.concatenate([place_ref[...], place_ref[...]], axis=0)
    for r in range(cycles):
        for copy in copies[r]:
            copy.wait()
        rows = [[] for _ in range(4)]
        for first in range(0, lev_count, 4):
            for j in range(2):
                at = slice(j * LANES, (j + 1) * LANES)
                low_half, high_half = [], []
                for level in (first, first + 2):
                    one, two = got_ref[r, level, :, at], got_ref[r, level + 1, :, at]
                    turned = pltpu.roll(jnp.where(half_lane, two, one), 64, 1)
                    low_half.append(jnp.where(half_lane, one, turned))
                    high_half.append(jnp.where(half_lane, turned, two))
                rows[2 * j].append(jnp.concatenate(low_half, axis=1))
                rows[2 * j + 1].append(jnp.concatenate(high_half, axis=1))
        high, low = split(jnp.concatenate([row for quads in rows for row in quads], axis=0))
        spread = jnp.dot(jnp.concatenate([high, low], axis=1), spread_by, preferred_element_type=jnp.float32)
        sets = lev_count // 4
        for q in range(4):
            total = spread[8 * sets * q : 8 * sets * q + 8]
            for i in range(1, sets):
                total = total + pltpu.roll(spread[8 * (sets * q + i) : 8 * (sets * q + i) + 8], 4 * fields * i, 1)
            total = jnp.take_along_axis(total, order, axis=0, mode="promise_in_bounds")
            begin = q * quarter * group
            size = min(quarter * group, span - begin)
            for k in range(8):
                s = (k % 2) * 4 + k // 2
                out_ref[r : r + 1, k * span + begin : k * span + begin + size] = total[s : s + 1, :size]


def local(spectral, legendre, slot_wave, cycle_len, lat_order):
    slot_count = spectral.shape[2]
    degrees = spectral.shape[3]
    half_cycles = legendre.shape[1]
    lev_count = lax.axis_size("lev")
    wave_count = lax.axis_size("wave")
    slots = slot_wave.shape[0]
    padded_len = (RMAX + 8 * lev_count - 1) // (8 * lev_count) * 8 * lev_count
    points_dev = padded_len // lev_count
    half_step = points_dev // 8
    parts = spectral.shape[0] * spectral.shape[1]
    fields = parts // 2
    cycles = lat_order.shape[0] // wave_count
    groups = (slot_count + LANES - 1) // LANES
    edge = max(BLOCK, slot_count // 5 // BLOCK * BLOCK)
    middle = max(0, slot_count - 2 * edge)
    chunks = [edge, middle // 2 // BLOCK * BLOCK]
    chunks += [middle - chunks[1], slot_count - edge - middle]
    chunks = [size for size in chunks if size > 0]
    packed = 0 < slot_count % LANES <= LANES // 2
    half_rows = 2 * lev_count
    counts = (half_step + 15) // 16
    low_at = (16 * counts + LANES - 1) // LANES * LANES

    quarter = (half_step + 3) // 4
    assert fields * quarter <= 64 and half_step <= LANES and lev_count % 4 == 0
    wide = 2 * LANES
    width = (quarter * fields * lev_count + LANES - 1) // LANES * LANES
    vmem = pl.BlockSpec(memory_space=pltpu.VMEM)
    hbm = pl.BlockSpec(memory_space=pl.ANY)
    return pl.pallas_call(
        functools.partial(kernel, half_step, tuple(chunks)),
        out_shape=pltpu.VMEM((cycles, points_dev * lev_count * fields), jnp.float32),
        in_specs=[hbm] * 5,
        out_specs=vmem,
        scratch_shapes=[
            pltpu.VMEM(slot_wave.shape, jnp.int32),
            pltpu.SMEM(lat_order.shape, jnp.int32),
            pltpu.SMEM(cycle_len.shape, jnp.int32),
            pltpu.VMEM((parts, slot_count, degrees), jnp.bfloat16),
            pltpu.VMEM((half_cycles, slot_count, degrees), jnp.bfloat16),
            pltpu.VMEM((groups * LANES, LANES), jnp.float32),
            pltpu.VMEM((2 * half_cycles, 8, LANES), jnp.float32),
            pltpu.VMEM((max(1, groups - packed), wave_count, cycles, 8, LANES), jnp.float32),
            pltpu.VMEM((max(1, groups - packed), wave_count, cycles, 8, LANES), jnp.float32),
            pltpu.VMEM((wave_count, cycles, 4, LANES), jnp.float32),
            pltpu.VMEM((wave_count, cycles, 4, LANES), jnp.float32),
            pltpu.VMEM((cycles, 2, slots // LANES, half_rows, LANES), jnp.float32),
            pltpu.VMEM((cycles, slots // LANES, 8, LANES), jnp.float32),
            pltpu.VMEM((cycles, 2, slots // LANES, low_at + 16 * counts, LANES), jnp.bfloat16),
            pltpu.VMEM((2 * LANES, width), jnp.bfloat16),
            pltpu.VMEM((cycles, lev_count, 8, wide), jnp.float32),
            pltpu.VMEM((cycles, lev_count, 8, wide), jnp.float32),
            pltpu.SemaphoreType.DMA((3,)),
            pltpu.SemaphoreType.DMA((2, len(chunks))),
            pltpu.SemaphoreType.DMA((groups,)),
            pltpu.SemaphoreType.DMA((groups, wave_count)),
            pltpu.SemaphoreType.DMA((groups, wave_count)),
            pltpu.SemaphoreType.DMA((cycles,)),
            pltpu.SemaphoreType.DMA((cycles, lev_count)),
            pltpu.SemaphoreType.DMA((cycles, lev_count)),
        ],
        compiler_params=pltpu.CompilerParams(collective_id=0, has_side_effects=True),
        name="transform",
    )(
        slot_wave, lat_order, cycle_len,
        spectral.reshape(parts, slot_count, degrees), jnp.transpose(legendre, (1, 0, 2)),
    )


def solution(mesh):
    in_specs = (P("lev", None, "wave", None), P("wave", None, None), P(), P(), P())
    out_specs = P("wave", "lev")
    return jax.shard_map(local, mesh=mesh, in_specs=in_specs, out_specs=out_specs, check_vma=False)
```
